256 devices in a mesh: band: 8 (over x, core), freq: 32 (over y, z).
Axes of the slice: x: 4, y: 4, z: 8, core: 2. Of those that a mesh axis runs over, the one named last changes fastest.
Arguments:
- spectrum: float32 [32, 36, 128, 256], P('freq', None, 'band'), may hold values from 0.05 to 1
- velocity: float32 [2, 24, 128, 256], P(None, None, 'band', 'freq'), may hold values from -3 to 3
- gain_matrix: bfloat16 [1152, 1152], replicated, may hold values from -0.1875 to 0.1875
- quad_matrix: bfloat16 [1152, 1152], replicated, may hold values from -0.1875 to 0.1875
- limiter_flags: int32 [8, 128, 256], replicated, may hold values 0 or 1
- sea_mask: int32 [128, 256], replicated, may hold values 0 or 1
- current_route: int32 [32], replicated, may hold values from 0 to 23
- stokes_route: int32 [32, 4], replicated, may hold values from 0 to 23
Outputs:
- spectrum_out: float32 [32, 36, 128, 256], P('freq', None, 'band')
- velocity_out: float32 [2, 24, 128, 256], P(None, None, 'band', 'freq')
The draws below stay inside these ranges and needn't reach their ends.
All inputs are finite; a program needn't handle non-finite values.
Results may differ from the reference program's by a relative error of at most 0.00045.
Values sent between devices are 32-bit elements; how exact they have to be, the bound alone decides.
No kernel may reach another device: no remote copies, remote signals or barrier semaphores. Data moves between devices by JAX's collectives and lax.ppermute only.
A program may use at most 64 MiB of HBM per device.

```python
import jax
import jax.numpy as jnp
from jax import lax

DIR = 36
LAT_DEV = 16
LAYERS = 24
SUB = 4
CYCLES = 2
OSTEPS = 3
KS = 4
F = 32
COMP = 1152
NLAT = 128
NLON = 256
N_BAND = 8


def place_ends(values, rng, least, top_value):
    place = [jax.random.randint(jax.random.fold_in(rng, axis), (), 0, length) for axis, length in enumerate(values.shape)]
    widest = values.shape.index(max(values.shape))
    next_to = place[:widest] + [(place[widest] + 1) % values.shape[widest]] + place[widest + 1:]
    return values.at[tuple(place)].set(least).at[tuple(next_to)].set(top_value)


def block_scale(stream_key, extent, cuts, least, high):
    loudness, own = 1.0, jax.random.fold_in(stream_key, 6)
    for axis_at, shards_of in cuts:
        heights = jnp.exp(jax.random.uniform(jax.random.fold_in(own, axis_at), (shards_of,), jnp.float32, least / len(cuts), high / len(cuts)))
        loudness = loudness * jnp.repeat(heights, extent[axis_at] // shards_of).reshape([-1 if axis == axis_at else 1 for axis in range(len(extent))])
    return loudness


def scatter_about(rng, dims, deviation, limit, pieces=(), kind=jnp.bfloat16):
    loudness = block_scale(rng, dims, pieces, -0.22, 0.18) if pieces else 1.0
    array = jax.random.normal(rng, dims, jnp.float32) * deviation * loudness
    return jnp.minimum(jnp.maximum(array, -limit), limit).astype(kind)


def setup_inputs(seed: int = 0) -> dict:
    seeds = jax.random.split(jax.random.key(seed), 9)
    spectrum = jnp.clip(0.05 + 0.95 * jax.random.uniform(seeds[0], (F, DIR, NLAT, NLON), jnp.float32) ** block_scale(seeds[0], (F, DIR, NLAT, NLON), ((0, 32), (2, 8)), -0.2, 0.2), 0.05, 1.0)
    velocity = scatter_about(seeds[1], (2, LAYERS, NLAT, NLON), 0.5, 3.0, ((2, 8), (3, 32)), jnp.float32)
    gain_matrix = scatter_about(seeds[2], (COMP, COMP), COMP ** -0.5, 0.1875)
    quad_matrix = scatter_about(seeds[3], (COMP, COMP), COMP ** -0.5, 0.1875)
    limiter_flags = place_ends((jax.random.randint(seeds[4], (CYCLES * SUB, NLAT, NLON), 0, 2) < 1).astype(jnp.int32), jax.random.fold_in(seeds[4], 1), 0, 1)
    sea_mask = place_ends((jax.random.randint(seeds[5], (NLAT, NLON), 0, 4) < 3).astype(jnp.int32), jax.random.fold_in(seeds[5], 1), 0, 1)
    current_route = place_ends(jax.random.randint(seeds[6], (F,), 0, LAYERS), jax.random.fold_in(seeds[6], 1), 0, LAYERS - 1).astype(jnp.int32)
    stokes_route = place_ends(jax.random.randint(seeds[7], (F, KS), 0, LAYERS), jax.random.fold_in(seeds[7], 1), 0, LAYERS - 1).astype(jnp.int32)
    return dict(spectrum=spectrum, velocity=velocity, gain_matrix=gain_matrix, quad_matrix=quad_matrix, limiter_flags=limiter_flags, sea_mask=sea_mask, current_route=current_route, stokes_route=stokes_route)


precise = lax.Precision.HIGHEST
ocean_dt = 0.2
viscous = 0.5
coriolis = 1.0
mixing = 0.5
friction = 0.1


def directions(how_many):
    angles = (jnp.arange(how_many, dtype=jnp.float32) + 0.5) * (2.0 * jnp.pi / how_many)
    return jnp.cos(angles), jnp.sin(angles)


def speed_of(position, total_count):
    return 0.5 + 0.3 * (position.astype(jnp.float32) + 0.5) / total_count


def wavenumber(position, total_count):
    return 0.5 + 1.5 * (position.astype(jnp.float32) + 0.5) / total_count


def pad_last(values):
    zero_col = jnp.zeros(values.shape[:-1] + (1,), values.dtype)
    return jnp.concatenate([zero_col, values, zero_col], axis=-1)


def transport(lower_side, upper_side, courant, limiter):
    upwind = jnp.maximum(courant, 0.0) * lower_side + jnp.minimum(courant, 0.0) * upper_side
    wendroff = 0.5 * courant * (lower_side + upper_side) - 0.5 * courant * courant * (upper_side - lower_side)
    return upwind + limiter * (wendroff - upwind)


def substep(extended, current, limiter_rows, sea_rows, rate_now, cos_table, sin_table):
    limiter = limiter_rows.astype(jnp.float32)
    drifts = 0.15 * jnp.tanh(current)
    north_drift = drifts[..., 1:2, :, :]
    face_north = 0.5 * (north_drift[..., :-1, :] + north_drift[..., 1:, :])
    courant = rate_now * sin_table[:, None, None] + face_north
    flux_north = transport(extended[..., :-1, :], extended[..., 1:, :], courant, limiter[1:, :])
    shifted = extended[..., 1:-1, :] - (flux_north[..., 1:, :] - flux_north[..., :-1, :])
    east_drift = pad_last(drifts[..., 0:1, 1:-1, :])
    face_east = 0.5 * (east_drift[..., :-1] + east_drift[..., 1:])
    courant_east = rate_now * cos_table[:, None, None] + face_east
    padded = pad_last(shifted)
    limiter_east = pad_last(limiter[1:-1, :])[:, 1:]
    flux_east = transport(padded[..., :-1], padded[..., 1:], courant_east, limiter_east)
    result = shifted - (flux_east[..., 1:] - flux_east[..., :-1])
    return result * sea_rows.astype(jnp.float32)


def source(block, gain_matrix, quad_matrix):
    block_shape = block.shape
    flattened = block.reshape(block_shape[0] * block_shape[1], -1)
    gain_arg = jnp.dot(gain_matrix, flattened.astype(jnp.bfloat16), preferred_element_type=jnp.float32)
    quartic = jnp.dot(quad_matrix, (flattened * flattened).astype(jnp.bfloat16), preferred_element_type=jnp.float32)
    updated = flattened * (1.0 + 0.5 * jnp.tanh(gain_arg) - 0.25 * jnp.tanh(quartic))
    return updated.reshape(block_shape)


def deposit_table(stokes_route):
    layer_ids = jnp.arange(LAYERS, dtype=jnp.int32)
    weights = 1.0 / (1.0 + jnp.arange(stokes_route.shape[1], dtype=jnp.float32))
    hits = (stokes_route[:, :, None] == layer_ids[None, None, :]).astype(jnp.float32)
    return jnp.sum(hits * weights[None, :, None], axis=1)


def stokes_profile(spectrum, numbers, deposit):
    cos_table, sin_table = directions(spectrum.shape[1])
    factor = numbers * (spectrum.shape[1] ** -0.5)
    eastward = jnp.einsum("fdrc,d->frc", spectrum, cos_table, precision=precise) * factor[:, None, None]
    northward = jnp.einsum("fdrc,d->frc", spectrum, sin_table, precision=precise) * factor[:, None, None]
    stacked = jnp.stack([eastward, northward], axis=1)
    return jnp.einsum("fl,fsrc->slrc", deposit, stacked, precision=precise)


def ocean_step(padded, stokes, sea_tile):
    inner = padded[:, :, 1:-1, 1:-1]
    laplace = padded[:, :, 2:, 1:-1] + padded[:, :, :-2, 1:-1] + padded[:, :, 1:-1, 2:] + padded[:, :, 1:-1, :-2] - 4.0 * inner
    vertical = jnp.pad(inner, ((0, 0), (1, 1), (0, 0), (0, 0)))
    mixing_term = vertical[:, 2:] + vertical[:, :-2] - 2.0 * inner
    moving = inner + stokes
    turning = jnp.stack([moving[1], -moving[0]])
    tendency = viscous * laplace + coriolis * turning + mixing * mixing_term - friction * inner
    return (inner + ocean_dt * tendency) * sea_tile.astype(jnp.float32)


def reference(spectrum, velocity, gain_matrix, quad_matrix, limiter_flags, sea_mask, current_route, stokes_route):
    freq_total = spectrum.shape[0]
    cos_table, sin_table = directions(DIR)
    indices = jnp.arange(freq_total, dtype=jnp.int32)
    speeds = speed_of(indices, freq_total)
    numbers = wavenumber(indices, freq_total)
    current = jnp.swapaxes(velocity[:, current_route], 0, 1)
    current_ext = jnp.pad(current, ((0, 0), (0, 0), (1, 1), (0, 0)))
    flag_ext = jnp.pad(limiter_flags, ((0, 0), (1, 1), (0, 0)))
    deposit = deposit_table(stokes_route)
    stokes = jnp.zeros((2, LAYERS) + spectrum.shape[2:], jnp.float32)
    for cycle_index in range(CYCLES):
        def advect(packed):
            field_now, drift_ext, rate_now = packed
            for step_index in range(SUB):
                extended = jnp.pad(field_now, ((0, 0), (1, 1), (0, 0)))
                field_now = substep(extended, drift_ext, flag_ext[cycle_index * SUB + step_index], sea_mask, rate_now, cos_table, sin_table)
            return field_now

        spectrum = lax.map(advect, (spectrum, current_ext, speeds))
        if cycle_index == 0:
            stokes = stokes_profile(spectrum, numbers, deposit)
        blocks = spectrum.reshape(freq_total, DIR, N_BAND, LAT_DEV, spectrum.shape[3])
        blocks = jnp.moveaxis(blocks, 2, 0)
        blocks = lax.map(lambda piece: source(piece, gain_matrix, quad_matrix), blocks)
        spectrum = jnp.moveaxis(blocks, 0, 2).reshape(freq_total, DIR, N_BAND * LAT_DEV, blocks.shape[-1])
    for step_index in range(OSTEPS):
        padded = jnp.pad(velocity, ((0, 0), (0, 0), (1, 1), (1, 1)))
        velocity = ocean_step(padded, stokes, sea_mask)
    return spectrum, velocity
```

```python
import jax
import jax.numpy as jnp
from jax import lax
from jax.sharding import PartitionSpec as P

DIR = 36
F_DEV = 1
LAYERS = 24
SUB = 4
CYCLES = 2
OSTEPS = 3


precise = lax.Precision.HIGHEST
ocean_dt = 0.2
viscous = 0.5
coriolis = 1.0
mixing = 0.5
friction = 0.1


def padded_2(cells, sides, width):
    for axis, dim in sides:
        count = lax.axis_size(axis)
        ends = count - 1
        head = lax.slice_in_dim(cells, 0, width, axis=dim)
        tail = lax.slice_in_dim(cells, cells.shape[dim] - width, cells.shape[dim], axis=dim)
        cells = jnp.concatenate(
            [
                lax.ppermute(tail, axis, [(i, (i + 1) % count) for i in range(ends)]),
                cells,
                lax.ppermute(head, axis, [((i + 1) % count, i) for i in range(ends)]),
            ],
            axis=dim,
        )
    return cells


def directions(how_many):
    angles = (jnp.arange(how_many, dtype=jnp.float32) + 0.5) * (2.0 * jnp.pi / how_many)
    return (jnp.cos(angles), jnp.sin(angles))


def speed_of(position, total_count):
    return 0.5 + 0.3 * (position.astype(jnp.float32) + 0.5) / total_count


def wavenumber(position, total_count):
    return 0.5 + 1.5 * (position.astype(jnp.float32) + 0.5) / total_count


def pad_last(values):
    zero_col = jnp.zeros(values.shape[:-1] + (1,), values.dtype)
    return jnp.concatenate([zero_col, values, zero_col], axis=-1)


def transport(lower_side, upper_side, courant, limiter):
    upwind = jnp.maximum(courant, 0.0) * lower_side + jnp.minimum(courant, 0.0) * upper_side
    wendroff = 0.5 * courant * (lower_side + upper_side) - 0.5 * courant * courant * (
        upper_side - lower_side
    )
    return upwind + limiter * (wendroff - upwind)


def substep(extended, current, limiter_rows, sea_rows, rate_now, cos_table, sin_table):
    limiter = limiter_rows.astype(jnp.float32)
    drifts = 0.15 * jnp.tanh(current)
    north_drift = drifts[..., 1:2, :, :]
    face_north = 0.5 * (north_drift[..., :-1, :] + north_drift[..., 1:, :])
    courant = rate_now * sin_table[:, None, None] + face_north
    flux_north = transport(extended[..., :-1, :], extended[..., 1:, :], courant, limiter[1:, :])
    shifted = extended[..., 1:-1, :] - (flux_north[..., 1:, :] - flux_north[..., :-1, :])
    east_drift = pad_last(drifts[..., 0:1, 1:-1, :])
    face_east = 0.5 * (east_drift[..., :-1] + east_drift[..., 1:])
    courant_east = rate_now * cos_table[:, None, None] + face_east
    padded = pad_last(shifted)
    limiter_east = pad_last(limiter[1:-1, :])[:, 1:]
    flux_east = transport(padded[..., :-1], padded[..., 1:], courant_east, limiter_east)
    result = shifted - (flux_east[..., 1:] - flux_east[..., :-1])
    return result * sea_rows.astype(jnp.float32)


def source(block, gain_matrix, quad_matrix):
    block_shape = block.shape
    flattened = block.reshape(block_shape[0] * block_shape[1], -1)
    gain_arg = jnp.dot(
        gain_matrix, flattened.astype(jnp.bfloat16), preferred_element_type=jnp.float32
    )
    quartic = jnp.dot(
        quad_matrix,
        (flattened * flattened).astype(jnp.bfloat16),
        preferred_element_type=jnp.float32,
    )
    updated = flattened * (1.0 + 0.5 * jnp.tanh(gain_arg) - 0.25 * jnp.tanh(quartic))
    return updated.reshape(block_shape)


def deposit_table(stokes_route):
    layer_ids = jnp.arange(LAYERS, dtype=jnp.int32)
    weights = 1.0 / (1.0 + jnp.arange(stokes_route.shape[1], dtype=jnp.float32))
    hits = (stokes_route[:, :, None] == layer_ids[None, None, :]).astype(jnp.float32)
    return jnp.sum(hits * weights[None, :, None], axis=1)


def stokes_profile(spectrum, numbers, deposit):
    cos_table, sin_table = directions(spectrum.shape[1])
    factor = numbers * spectrum.shape[1] ** (-0.5)
    eastward = (
        jnp.einsum("fdrc,d->frc", spectrum, cos_table, precision=precise) * factor[:, None, None]
    )
    northward = (
        jnp.einsum("fdrc,d->frc", spectrum, sin_table, precision=precise) * factor[:, None, None]
    )
    stacked = jnp.stack([eastward, northward], axis=1)
    return jnp.einsum("fl,fsrc->slrc", deposit, stacked, precision=precise)


def ocean_step(padded, stokes, sea_tile):
    inner = padded[:, :, 1:-1, 1:-1]
    laplace = (
        padded[:, :, 2:, 1:-1]
        + padded[:, :, :-2, 1:-1]
        + padded[:, :, 1:-1, 2:]
        + padded[:, :, 1:-1, :-2]
        - 4.0 * inner
    )
    vertical = jnp.pad(inner, ((0, 0), (1, 1), (0, 0), (0, 0)))
    mixing_term = vertical[:, 2:] + vertical[:, :-2] - 2.0 * inner
    moving = inner + stokes
    turning = jnp.stack([moving[1], -moving[0]])
    tendency = viscous * laplace + coriolis * turning + mixing * mixing_term - friction * inner
    return (inner + ocean_dt * tendency) * sea_tile.astype(jnp.float32)


def body(
    spectrum,
    velocity,
    gain_matrix,
    quad_matrix,
    limiter_flags,
    sea_mask,
    current_route,
    stokes_route,
):
    band_index = lax.axis_index("band")
    freq_index = lax.axis_index("freq")
    freq_count = lax.axis_size("freq")
    freq_total = F_DEV * freq_count
    local_rows = spectrum.shape[2]
    grid_cols = spectrum.shape[3]
    tile_cols = velocity.shape[3]
    cos_table, sin_table = directions(DIR)
    own_freqs = freq_index * F_DEV + jnp.arange(F_DEV, dtype=jnp.int32)
    rate_now = speed_of(own_freqs, freq_total).reshape(F_DEV, 1, 1, 1)
    deposit_all = deposit_table(stokes_route)
    layer_ids = jnp.arange(LAYERS, dtype=jnp.int32)
    picker = (current_route[:, None] == layer_ids[None, :]).astype(jnp.float32)
    outgoing = jnp.einsum("fl,slrc->fsrc", picker, velocity, precision=precise)
    current = lax.all_to_all(outgoing, "freq", split_axis=0, concat_axis=3, tiled=True)
    depth = 1
    current_ext = padded_2(current, (("band", 2),), depth)
    flag_pad = jnp.pad(limiter_flags, ((0, 0), (SUB, SUB), (0, 0)))
    sea_pad = jnp.pad(sea_mask, ((SUB, SUB), (0, 0)))
    row_base = band_index * local_rows + SUB
    field_now = spectrum
    drift_tile = None
    for cycle_index in range(CYCLES):
        for step_index in range(SUB):
            extended = padded_2(field_now, (("band", 2),), 1)
            flag_rows = lax.dynamic_slice_in_dim(
                flag_pad[cycle_index * SUB + step_index], row_base - 1, local_rows + 2 * 1, 0
            )
            sea_rows = lax.dynamic_slice_in_dim(
                sea_pad, row_base - 1 + 1, local_rows + 2 * 1 - 2, 0
            )
            field_now = substep(
                extended, current_ext, flag_rows, sea_rows, rate_now, cos_table, sin_table
            )
        grouped = field_now.reshape(F_DEV, DIR, local_rows, freq_count, tile_cols)
        grouped = jnp.transpose(grouped, (0, 1, 3, 2, 4)).reshape(
            F_DEV, DIR, freq_count, local_rows * tile_cols
        )
        cells = lax.all_to_all(grouped, "freq", split_axis=2, concat_axis=0, tiled=True)
        if cycle_index == 0:
            numbers = wavenumber(jnp.arange(freq_total, dtype=jnp.int32), freq_total)
            drift_tile = stokes_profile(cells, numbers, deposit_all)
            drift_tile = drift_tile.reshape(2, LAYERS, local_rows, tile_cols)
        whole = source(cells, gain_matrix, quad_matrix)
        moved = lax.all_to_all(whole, "freq", split_axis=0, concat_axis=2, tiled=True)
        moved = moved.reshape(F_DEV, DIR, freq_count, local_rows, tile_cols)
        field_now = jnp.transpose(moved, (0, 1, 3, 2, 4)).reshape(F_DEV, DIR, local_rows, grid_cols)
    sea_tile = lax.dynamic_slice(
        sea_mask, (band_index * local_rows, freq_index * tile_cols), (local_rows, tile_cols)
    )
    ocean_now = velocity
    for step_index in range(OSTEPS):
        padded = padded_2(ocean_now, (("band", 2), ("freq", 3)), 1)
        ocean_now = ocean_step(padded, drift_tile, sea_tile)
    return (field_now, ocean_now)


def solution(mesh):
    return jax.shard_map(
        body,
        mesh=mesh,
        in_specs=(
            P("freq", None, "band", None),
            P(None, None, "band", "freq"),
            P(),
            P(),
            P(),
            P(),
            P(),
            P(),
        ),
        out_specs=(P("freq", None, "band", None), P(None, None, "band", "freq")),
        check_vma=False,
    )
```

```python
import jax
import jax.numpy as jnp
from jax import lax
from jax.experimental import pallas as pl
from jax.experimental.pallas import tpu as pltpu
from jax.sharding import PartitionSpec as P

DIR = 36
FREQS = 32
COMP = 1152
LAYERS = 24
SUB = 4
CYCLES = 2
OSTEPS = 3
BANDS = 8
ROWS = 16
COLS = 8
HALO = 4
EXT_R = 24
EXT_C = 16
LANES = 128
GROUPS = 9

precise = lax.Precision.HIGHEST
ocean_dt = 0.2
viscous = 0.5
mixing = 0.5
friction = 0.1

SIDES = ((0, 1), (0, -1), (1, 0), (-1, 0), (1, 1), (1, -1), (-1, 1), (-1, -1))
f32 = jnp.float32


def directions(how_many):
    angles = (jnp.arange(how_many, dtype=f32) + 0.5) * (2.0 * jnp.pi / how_many)
    return (jnp.cos(angles), jnp.sin(angles))


def speed_of(position, total_count):
    return 0.5 + 0.3 * (position.astype(f32) + 0.5) / total_count


def wavenumber(position, total_count):
    return 0.5 + 1.5 * (position.astype(f32) + 0.5) / total_count


def deposit_table(stokes_route):
    layer_ids = jnp.arange(LAYERS, dtype=jnp.int32)
    weights = 1.0 / (1.0 + jnp.arange(stokes_route.shape[1], dtype=f32))
    hits = (stokes_route[:, :, None] == layer_ids[None, None, :]).astype(f32)
    return jnp.sum(hits * weights[None, :, None], axis=1)


def sent_rows(side):
    return {0: (0, ROWS), 1: (0, HALO), -1: (ROWS - HALO, ROWS)}[side]


def sent_cols(side):
    return {0: (0, COLS), 1: (0, HALO), -1: (COLS - HALO, COLS)}[side]


def kept_rows(side):
    return {0: HALO, 1: HALO + ROWS, -1: 0}[side]


def kept_cols(side):
    return {0: (0, COLS), 1: (COLS, COLS + HALO), -1: (COLS + HALO, EXT_C)}[side]


def message_shape(side, lanes):
    return (ROWS if side[0] == 0 else HALO, COLS if side[1] == 0 else HALO, lanes)


def exchange(messages):
    received = []
    for (db, dt), message in zip(SIDES, messages):
        pairs = [
            ((b + db) * FREQS + t + dt, b * FREQS + t)
            for b in range(BANDS)
            for t in range(FREQS)
            if 0 <= b + db < BANDS and 0 <= t + dt < FREQS
        ]
        received.append(lax.ppermute(message, ("band", "freq"), pairs))
    return received


def swap_blocks(tiles):
    block = lax.broadcasted_iota(jnp.int32, tiles[0].shape, 1) // 8
    for bit in (1, 2, 4, 8):
        upper = (block & bit) != 0
        fresh = list(tiles)
        for low in range(16):
            if low & bit:
                continue
            high = low | bit
            fresh[low] = jnp.where(upper, pltpu.roll(tiles[high], bit * 8, 1), tiles[low])
            fresh[high] = jnp.where(upper, tiles[high], pltpu.roll(tiles[low], LANES - bit * 8, 1))
        tiles = fresh
    return tiles


def spread_kernel(x_ref, o_ref, half_ref):
    for half in range(2):
        half_ref[half] = x_ref[:, half * LANES : (half + 1) * LANES]
        for first in range(0, DIR, 8):
            count = min(8, DIR - first)
            tiles = [half_ref[half, pl.ds(first * ROWS + r, count, stride=ROWS), :] for r in range(16)]
            for i, tile in enumerate(swap_blocks(tiles)):
                o_ref[half * 16 + i, pl.ds(first, count), :] = tile


def gather_kernel(x_ref, o_ref, half_ref):
    for half in range(2):
        for first in range(0, DIR, 8):
            count = min(8, DIR - first)
            tiles = [x_ref[half * 16 + i, pl.ds(first, count), :] for i in range(16)]
            for r, tile in enumerate(swap_blocks(tiles)):
                half_ref[half, pl.ds(first * ROWS + r, count, stride=ROWS), :] = tile
        o_ref[:, half * LANES : (half + 1) * LANES] = half_ref[half]


def put_messages(value, message_refs, lanes):
    for side, ref in zip(SIDES, message_refs):
        r0, r1 = sent_rows(side[0])
        c0, c1 = sent_cols(side[1])
        ref[:, :, lanes] = value[r0:r1, c0:c1, :]


def unpack_kernel(x_ref, c_ref, *rest):
    message_refs, flat_ref = rest[:-1], rest[-1]
    for g in range(FREQS):
        flat_ref[pl.ds(g * DIR, DIR), :] = x_ref[g]
    for k in range(GROUPS):
        lanes = pl.ds(k * LANES, LANES)
        tile = jnp.transpose(flat_ref[lanes, :]).reshape(ROWS, COLS, LANES)
        c_ref[:, :, lanes] = tile
        put_messages(tile, message_refs, lanes)


def face_flux(lower, upper, half_courant, second):
    q = jnp.where(second, (half_courant + half_courant) * half_courant, jnp.abs(half_courant))
    return lower * (half_courant + q) + upper * (half_courant - q)


def cycle_kernel(first, *refs):
    refs = list(refs)
    take = lambda n: [refs.pop(0) for _ in range(n)]
    (c_ref,) = take(1)
    message_refs = take(8)
    north_ref, east_ref, flag_ref, sea_ref, gain_hbm, quad_hbm = take(6)
    if first:
        weight_hi, weight_lo, out_ref, stokes_ref = take(4)
        out_refs = take(8)
    else:
        (out_ref,) = take(1)
    tile_ref, energy_ref, gain_ref, quad_ref, sems = take(5)
    copies = [
        pltpu.make_async_copy(gain_hbm, gain_ref, sems.at[0]),
        pltpu.make_async_copy(quad_hbm, quad_ref, sems.at[1]),
    ]
    for copy in copies:
        copy.start()

    def advect(k, carry):
        lanes = pl.ds(pl.multiple_of(k * LANES, LANES), LANES)
        tile_ref[HALO : HALO + ROWS, 0:COLS, :] = c_ref[:, :, lanes]
        for side, ref in zip(SIDES, message_refs):
            r0 = kept_rows(side[0])
            c0, c1 = kept_cols(side[1])
            tile_ref[r0 : r0 + ref.shape[0], c0:c1, :] = ref[:, :, lanes]
        for s in range(SUB):
            here = tile_ref[s]
            above = tile_ref[s + 1]
            flag = flag_ref[s, s + 1] != 0.0
            flux_below = face_flux(here, above, north_ref[s, :, lanes], flag)
            for r in range(s + 1, EXT_R - 1 - s):
                here = above
                above = tile_ref[r + 1]
                flag_above = flag_ref[s, r + 1] != 0.0
                flux_above = face_flux(here, above, north_ref[r, :, lanes], flag_above)
                shifted = here - (flux_above - flux_below)
                flux_east = face_flux(
                    pltpu.roll(shifted, 1, 0), shifted, east_ref[r, :, lanes], flag
                )
                result = shifted - (pltpu.roll(flux_east, EXT_C - 1, 0) - flux_east)
                result = result * sea_ref[r]
                if s == SUB - 1:
                    energy_ref[r - HALO, :, lanes] = result[0:COLS]
                else:
                    tile_ref[r] = result
                flux_below = flux_above
                flag = flag_above
        return carry

    lax.fori_loop(0, GROUPS, advect, 0)
    cells = ROWS * COLS
    energy = energy_ref[...].reshape(cells, COMP)
    rounded = energy.astype(jnp.bfloat16)
    squared = (energy * energy).astype(jnp.bfloat16)
    if first:
        rest = (energy - rounded.astype(f32)).astype(jnp.bfloat16)
        mm = lambda a, b: jnp.dot(a, b, preferred_element_type=f32)
        stokes = mm(rounded, weight_hi[...]) + (mm(rest, weight_hi[...]) + mm(rounded, weight_lo[...]))
        stokes = stokes.reshape(ROWS, COLS, LANES)
        stokes_ref[...] = stokes
        put_messages(stokes, out_refs, pl.ds(COMP, LANES))
    for copy in copies:
        copy.wait()
    nt = (((1,), (1,)), ((), ()))
    for k in range(GROUPS):
        lanes = pl.ds(k * LANES, LANES)
        gain = lax.dot_general(rounded, gain_ref[lanes, :], nt, preferred_element_type=f32)
        quartic = lax.dot_general(squared, quad_ref[lanes, :], nt, preferred_element_type=f32)
        before = energy_ref[:, :, lanes].reshape(cells, LANES)
        updated = before * (1.0 + 0.5 * jnp.tanh(gain) - 0.25 * jnp.tanh(quartic))
        if first:
            updated = updated.reshape(ROWS, COLS, LANES)
            out_ref[:, :, lanes] = updated
            put_messages(updated, out_refs, lanes)
        else:
            flat = jnp.transpose(updated)
            start = k * LANES
            while start < (k + 1) * LANES:
                g, d = divmod(start, DIR)
                count = min(DIR - d, (k + 1) * LANES - start)
                at = start - k * LANES
                out_ref[g, d : d + count, :] = flat[at : at + count, :]
                start += count


def ocean_kernel(u_ref, stokes_ref, *refs):
    message_refs, (sea_ref, o_ref, now_ref, drift_ref) = refs[:8], refs[8:]
    now_ref[...] = u_ref[...]
    drift_ref[HALO : HALO + ROWS, 0:COLS, :] = stokes_ref[...]
    for side, ref in zip(SIDES, message_refs):
        r0 = kept_rows(side[0])
        c0, c1 = kept_cols(side[1])
        drift_ref[r0 : r0 + ref.shape[0], c0:c1, :] = ref[...]
    lane = lax.broadcasted_iota(jnp.int32, (EXT_C, LANES), 1)
    used = lane < 2 * LAYERS
    east = lane < LAYERS
    top = (lane == LAYERS - 1) | (lane == 2 * LAYERS - 1)
    bottom = (lane == 0) | (lane == LAYERS)
    for s in range(OSTEPS):
        low = 2 + s
        below = now_ref[low - 1]
        here = now_ref[low]
        for r in range(low, EXT_R - low):
            above = now_ref[r + 1]
            laplace = above + below + pltpu.roll(here, EXT_C - 1, 0) + pltpu.roll(here, 1, 0) - 4.0 * here
            moving = here + drift_ref[r]
            turning = jnp.where(
                east, pltpu.roll(moving, LANES - LAYERS, 1), -pltpu.roll(moving, LAYERS, 1)
            )
            over = jnp.where(top, 0.0, pltpu.roll(here, LANES - 1, 1))
            under = jnp.where(bottom, 0.0, pltpu.roll(here, 1, 1))
            tendency = (
                viscous * laplace + turning + mixing * (over + under - 2.0 * here) - friction * here
            )
            result = jnp.where(used, (here + ocean_dt * tendency) * sea_ref[r], 0.0)
            if s == OSTEPS - 1:
                o_ref[r - HALO] = result[0:COLS]
            else:
                now_ref[r] = result
            below, here = here, above


def shape_of(*dims, dtype=f32):
    return jax.ShapeDtypeStruct(dims, dtype)


vmem = pl.BlockSpec(memory_space=pltpu.VMEM)
hbm = pl.BlockSpec(memory_space=pl.ANY)
big = pltpu.CompilerParams(vmem_limit_bytes=40 * 2**20)


def spread(x):
    return pl.pallas_call(
        spread_kernel,
        out_shape=shape_of(FREQS, DIR, LANES),
        in_specs=[vmem],
        out_specs=vmem,
        scratch_shapes=[pltpu.VMEM((2, DIR * ROWS, LANES), f32)],
        name="spread",
    )(x.reshape(DIR * ROWS, 2 * LANES))


def collect(x):
    return pl.pallas_call(
        gather_kernel,
        out_shape=shape_of(DIR * ROWS, 2 * LANES),
        in_specs=[vmem],
        out_specs=vmem,
        scratch_shapes=[pltpu.VMEM((2, DIR * ROWS, LANES), f32)],
        name="collect",
    )(x).reshape(1, DIR, ROWS, 2 * LANES)


def unpack(x):
    out = pl.pallas_call(
        unpack_kernel,
        out_shape=[shape_of(ROWS, COLS, COMP)] + [shape_of(*message_shape(s, COMP)) for s in SIDES],
        in_specs=[vmem],
        out_specs=[vmem] * 9,
        scratch_shapes=[pltpu.VMEM((COMP, LANES), f32)],
        name="unpack",
    )(x)
    return out[0], out[1:]


def run_cycle(first, cells, halos, north, east, flags, sea, gain, quad, weights):
    operands = [cells, *halos, north, east, flags, sea, gain, quad]
    if first:
        operands += weights
        out_shape = [shape_of(ROWS, COLS, COMP), shape_of(ROWS, COLS, LANES)]
        out_shape += [shape_of(*message_shape(s, COMP + LANES)) for s in SIDES]
    else:
        out_shape = [shape_of(FREQS, DIR, LANES)]
    specs = [vmem] * len(operands)
    specs[13] = hbm
    specs[14] = hbm
    return pl.pallas_call(
        lambda *refs: cycle_kernel(first, *refs),
        out_shape=out_shape,
        in_specs=specs,
        out_specs=[vmem] * len(out_shape),
        scratch_shapes=[
            pltpu.VMEM((EXT_R, EXT_C, LANES), f32),
            pltpu.VMEM((ROWS, COLS, COMP), f32),
            pltpu.VMEM((COMP, COMP), jnp.bfloat16),
            pltpu.VMEM((COMP, COMP), jnp.bfloat16),
            pltpu.SemaphoreType.DMA((2,)),
        ],
        compiler_params=big,
        name="cycle_first" if first else "cycle_last",
    )(*operands)


def ocean(velocity_ext, stokes, halos, sea):
    operands = [velocity_ext, stokes, *halos, sea]
    return pl.pallas_call(
        ocean_kernel,
        out_shape=shape_of(ROWS, COLS, LANES),
        in_specs=[vmem] * len(operands),
        out_specs=vmem,
        scratch_shapes=[pltpu.VMEM((EXT_R, EXT_C, LANES), f32)] * 2,
        name="ocean",
    )(*operands)


def line(count, shift):
    return [(i, i - shift) for i in range(count) if 0 <= i - shift < count]


def body(
    spectrum,
    velocity,
    gain_matrix,
    quad_matrix,
    limiter_flags,
    sea_mask,
    current_route,
    stokes_route,
):
    band_index = lax.axis_index("band")
    freq_index = lax.axis_index("freq")
    chunks = lax.all_to_all(spread(spectrum), "freq", split_axis=0, concat_axis=0, tiled=True)

    tile = jnp.transpose(velocity, (2, 3, 0, 1)).reshape(ROWS, COLS, 2 * LAYERS)
    from_next = lax.ppermute(tile[:, :HALO], "freq", line(FREQS, 1))
    from_last = lax.ppermute(tile[:, HALO:], "freq", line(FREQS, -1))
    wide = jnp.concatenate([tile, from_next, from_last], axis=1)
    from_up = lax.ppermute(wide[:HALO], "band", line(BANDS, 1))
    from_down = lax.ppermute(wide[-HALO:], "band", line(BANDS, -1))
    velocity_ext = jnp.concatenate([from_down, wide, from_up], axis=0)

    drift = 0.15 * jnp.tanh(velocity_ext)
    drift_east = drift[..., :LAYERS]
    drift_north = drift[..., LAYERS:]
    half_east = 0.25 * (drift_east + jnp.roll(drift_east, 1, axis=1))
    half_north = 0.25 * (drift_north + jnp.roll(drift_north, -1, axis=0))
    layer_ids = jnp.arange(LAYERS, dtype=jnp.int32)
    routes = jnp.repeat(current_route, DIR)
    picker = (layer_ids[:, None] == routes[None, :]).astype(f32)
    cos_table, sin_table = directions(DIR)
    speeds = speed_of(jnp.arange(FREQS, dtype=jnp.int32), FREQS)
    half_cos = 0.5 * (speeds[:, None] * cos_table[None, :]).reshape(COMP)
    half_sin = 0.5 * (speeds[:, None] * sin_table[None, :]).reshape(COMP)
    pick = lambda x: jnp.einsum("rcl,lk->rck", x, picker, precision=precise)
    north = half_sin + pick(half_north)
    east = half_cos + pick(half_east)

    def window(grid):
        padded = jnp.pad(grid, ((0, 0), (HALO, HALO), (HALO, HALO))).astype(f32)
        part = lax.dynamic_slice(
            padded,
            (0, band_index * ROWS, freq_index * COLS),
            (grid.shape[0], EXT_R, EXT_C),
        )
        part = jnp.concatenate([part[:, :, HALO:], part[:, :, :HALO]], axis=2)
        return jnp.broadcast_to(part[..., None], part.shape + (LANES,))

    flags = window(limiter_flags)
    sea = window(sea_mask[None])[0]

    numbers = wavenumber(jnp.arange(FREQS, dtype=jnp.int32), FREQS) * DIR ** (-0.5)
    deposit = deposit_table(stokes_route) * numbers[:, None]
    both = jnp.stack([cos_table, sin_table])
    weight = (both.T[None, :, :, None] * deposit[:, None, None, :]).reshape(COMP, 2 * LAYERS)
    weight = jnp.pad(weight, ((0, 0), (0, LANES - 2 * LAYERS)))
    weight_hi = lax.reduce_precision(weight, 8, 7)
    weight_lo = (weight - weight_hi).astype(jnp.bfloat16)
    weights = [weight_hi.astype(jnp.bfloat16), weight_lo]

    cells, messages = unpack(chunks)
    halos = exchange(messages)
    results = run_cycle(
        True, cells, halos, north, east, flags[:SUB], sea, gain_matrix, quad_matrix, weights
    )
    cells, stokes, messages = results[0], results[1], results[2:]
    halos = exchange(messages)
    (chunks,) = run_cycle(
        False, cells, halos, north, east, flags[SUB:], sea, gain_matrix, quad_matrix, None
    )
    chunks = lax.all_to_all(chunks, "freq", split_axis=0, concat_axis=0, tiled=True)
    velocity_wide = jnp.pad(velocity_ext, ((0, 0), (0, 0), (0, LANES - 2 * LAYERS)))
    ocean_out = ocean(velocity_wide, stokes, [h[:, :, COMP:] for h in halos], sea)
    ocean_out = ocean_out[:, :, : 2 * LAYERS].reshape(ROWS, COLS, 2, LAYERS)
    velocity_out = jnp.transpose(ocean_out, (2, 3, 0, 1))
    return (collect(chunks), velocity_out)


def solution(mesh):
    return jax.shard_map(
        body,
        mesh=mesh,
        in_specs=(
            P("freq", None, "band", None),
            P(None, None, "band", "freq"),
            P(),
            P(),
            P(),
            P(),
            P(),
            P(),
        ),
        out_specs=(P("freq", None, "band", None), P(None, None, "band", "freq")),
        check_vma=False,
    )
```

```python
import jax
import jax.numpy as jnp
from jax import lax
from jax.experimental import pallas as pl
from jax.experimental.pallas import tpu as pltpu
from jax.sharding import PartitionSpec as P

DIR = 36
FREQS = 32
COMP = 1152
LAYERS = 24
SUB = 4
CYCLES = 2
OSTEPS = 3
BANDS = 8
ROWS = 16
COLS = 8
HALO = 4
EXT_R = 24
EXT_C = 16
LANES = 128
GROUPS = 9
WIDE = COMP + LANES

precise = lax.Precision.HIGHEST
ocean_dt = 0.2
viscous = 0.5
mixing = 0.5
friction = 0.1

f32 = jnp.float32


def directions(how_many):
    angles = (jnp.arange(how_many, dtype=f32) + 0.5) * (2.0 * jnp.pi / how_many)
    return (jnp.cos(angles), jnp.sin(angles))


def speed_of(position, total_count):
    return 0.5 + 0.3 * (position.astype(f32) + 0.5) / total_count


def wavenumber(position, total_count):
    return 0.5 + 1.5 * (position.astype(f32) + 0.5) / total_count


def deposit_table(stokes_route):
    layer_ids = jnp.arange(LAYERS, dtype=jnp.int32)
    weights = 1.0 / (1.0 + jnp.arange(stokes_route.shape[1], dtype=f32))
    hits = (stokes_route[:, :, None] == layer_ids[None, None, :]).astype(f32)
    return jnp.sum(hits * weights[None, :, None], axis=1)


def line(count, shift):
    return [(i, i - shift) for i in range(count) if 0 <= i - shift < count]


def widen(own, to_last, to_next):
    from_next = lax.ppermute(to_last, "freq", line(FREQS, 1))
    from_last = lax.ppermute(to_next, "freq", line(FREQS, -1))
    first, last = ends(own, from_next, from_last)
    from_up = lax.ppermute(first, "band", line(BANDS, 1))
    from_down = lax.ppermute(last, "band", line(BANDS, -1))
    return [own, from_next, from_last, from_up, from_down]


def fill(ext_ref, pieces, lanes):
    own, from_next, from_last, from_up, from_down = pieces
    middle = slice(HALO, HALO + ROWS)
    ext_ref[middle, 0:COLS, :] = own[:, :, lanes]
    ext_ref[middle, COLS : COLS + HALO, :] = from_next[:, :, lanes]
    ext_ref[middle, COLS + HALO : EXT_C, :] = from_last[:, :, lanes]
    ext_ref[HALO + ROWS : EXT_R] = from_up[:, :, lanes]
    ext_ref[0:HALO] = from_down[:, :, lanes]


def swap_blocks(tiles):
    block = lax.broadcasted_iota(jnp.int32, tiles[0].shape, 1) // 8
    for bit in (1, 2, 4, 8):
        upper = (block & bit) != 0
        fresh = list(tiles)
        for low in range(16):
            if low & bit:
                continue
            high = low | bit
            fresh[low] = jnp.where(upper, pltpu.roll(tiles[high], bit * 8, 1), tiles[low])
            fresh[high] = jnp.where(upper, tiles[high], pltpu.roll(tiles[low], LANES - bit * 8, 1))
        tiles = fresh
    return tiles


def spread_kernel(x_ref, o_ref, half_ref):
    for half in range(2):
        half_ref[half] = x_ref[:, half * LANES : (half + 1) * LANES]
        tiles = [half_ref[half, pl.ds(r, 8, stride=ROWS), :] for r in range(ROWS)]
        for i, tile in enumerate(swap_blocks(tiles)):
            o_ref[half * ROWS + i] = tile


def collect_kernel(x_ref, o_ref, half_ref):
    for half in range(2):
        tiles = [x_ref[half * ROWS + i] for i in range(ROWS)]
        for r, tile in enumerate(swap_blocks(tiles)):
            half_ref[half, pl.ds(r, 8, stride=ROWS), :] = tile
        o_ref[:, half * LANES : (half + 1) * LANES] = half_ref[half]


def ends_kernel(own, from_next, from_last, first_ref, last_ref):
    for ref, rows in ((first_ref, slice(0, HALO)), (last_ref, slice(ROWS - HALO, ROWS))):
        ref[:, 0:COLS, :] = own[rows]
        ref[:, COLS : COLS + HALO, :] = from_next[rows]
        ref[:, COLS + HALO : EXT_C, :] = from_last[rows]


def put(value, refs, lanes):
    refs[0][:, :, lanes] = value
    refs[1][:, :, lanes] = value[:, :HALO, :]
    refs[2][:, :, lanes] = value[:, HALO:, :]


def unpack_kernel(x_ref, u_ref, *rest):
    out_refs, flat_ref = rest[:-1], rest[-1]
    for g in range(FREQS):
        flat_ref[pl.ds(g * DIR, DIR), :] = x_ref[g]
    for k in range(GROUPS):
        lanes = slice(k * LANES, (k + 1) * LANES)
        put(jnp.transpose(flat_ref[lanes, :]).reshape(ROWS, COLS, LANES), out_refs, lanes)
    put(u_ref[...], out_refs, slice(COMP, WIDE))


def face_flux(lower, upper, half_courant, second):
    q = jnp.where(second, (half_courant + half_courant) * half_courant, jnp.abs(half_courant))
    return lower * (half_courant + q) + upper * (half_courant - q)


def courants(ext_ref, lane_ref, pick_ref, north_ref, east_ref):
    lane = lax.broadcasted_iota(jnp.int32, (EXT_C, LANES), 1)
    quarter = (0.25 * 0.15) * jnp.tanh(ext_ref[...])
    faces = []
    for r in range(EXT_R):
        along_rows = quarter[r] + quarter[min(r + 1, EXT_R - 1)]
        along_cols = quarter[r] + pltpu.roll(quarter[r], 1, 0)
        faces.append(jnp.where(lane < LAYERS, along_cols, along_rows))
    faces = jnp.concatenate(faces, axis=0)
    high = faces.astype(jnp.bfloat16)
    rest = faces - high.astype(f32)
    middle = rest.astype(jnp.bfloat16)
    low = (rest - middle.astype(f32)).astype(jnp.bfloat16)
    parts = jnp.concatenate([high, middle, low], axis=1)
    for index, ref in ((0, east_ref), (1, north_ref)):
        picked = jnp.dot(parts, pick_ref[index], preferred_element_type=f32)
        ref[...] = (lane_ref[index] + picked).reshape(EXT_R, EXT_C, COMP)


def cycle_kernel(first, *refs):
    refs = list(refs)
    take = lambda n: [refs.pop(0) for _ in range(n)]
    pieces = take(5)
    flag_ref, sea_ref, gain_ref, quad_ref = take(4)
    if first:
        lane_ref, pick_ref, weight_hi, weight_lo = take(4)
        out_refs = take(3)
        ext_ref, north_ref, east_ref = take(3)
    else:
        north_ref, east_ref = take(2)
        out_ref, ext_ref = take(2)
    tile_ref, energy_ref = take(2)
    fill(ext_ref, pieces, slice(COMP, WIDE))
    if first:
        courants(ext_ref, lane_ref, pick_ref, north_ref, east_ref)

    def advect(k, carry):
        lanes = pl.ds(pl.multiple_of(k * LANES, LANES), LANES)
        fill(tile_ref, pieces, lanes)
        for s in range(SUB):
            here = tile_ref[s]
            above = tile_ref[s + 1]
            flag = flag_ref[s, s + 1] != 0.0
            flux_below = face_flux(here, above, north_ref[s, :, lanes], flag)
            for r in range(s + 1, EXT_R - 1 - s):
                here = above
                above = tile_ref[r + 1]
                flag_above = flag_ref[s, r + 1] != 0.0
                flux_above = face_flux(here, above, north_ref[r, :, lanes], flag_above)
                shifted = here - (flux_above - flux_below)
                flux_east = face_flux(
                    pltpu.roll(shifted, 1, 0), shifted, east_ref[r, :, lanes], flag
                )
                result = shifted - (pltpu.roll(flux_east, EXT_C - 1, 0) - flux_east)
                result = result * sea_ref[r]
                if s == SUB - 1:
                    energy_ref[r - HALO, :, lanes] = result[0:COLS]
                else:
                    tile_ref[r] = result
                flux_below = flux_above
                flag = flag_above
        return carry

    lax.fori_loop(0, GROUPS, advect, 0)
    cells = ROWS * COLS
    energy = energy_ref[...].reshape(cells, COMP)
    rounded = energy.astype(jnp.bfloat16)
    squared = (energy * energy).astype(jnp.bfloat16)
    if first:
        rest = (energy - rounded.astype(f32)).astype(jnp.bfloat16)
        mm = lambda a, b: jnp.dot(a, b, preferred_element_type=f32)
        stokes = mm(rounded, weight_hi[...]) + (mm(rest, weight_hi[...]) + mm(rounded, weight_lo[...]))
        stokes = stokes.reshape(ROWS, COLS, LANES)
        put(stokes, out_refs, pl.ds(COMP, LANES))
    nt = (((1,), (1,)), ((), ()))
    for k in range(GROUPS):
        lanes = pl.ds(k * LANES, LANES)
        gain = lax.dot_general(rounded, gain_ref[lanes, :], nt, preferred_element_type=f32)
        quartic = lax.dot_general(squared, quad_ref[lanes, :], nt, preferred_element_type=f32)
        before = energy_ref[:, :, lanes].reshape(cells, LANES)
        updated = before * (1.0 + 0.5 * jnp.tanh(gain) - 0.25 * jnp.tanh(quartic))
        if first:
            put(updated.reshape(ROWS, COLS, LANES), out_refs, lanes)
        else:
            flat = jnp.transpose(updated)
            start = k * LANES
            while start < (k + 1) * LANES:
                g, d = divmod(start, DIR)
                count = min(DIR - d, (k + 1) * LANES - start)
                at = start - k * LANES
                out_ref[g, d : d + count, :] = flat[at : at + count, :]
                start += count


def ocean_kernel(u_ref, drift_ref, sea_ref, o_ref, now_ref):
    now_ref[...] = u_ref[...]
    lane = lax.broadcasted_iota(jnp.int32, (EXT_C, LANES), 1)
    used = lane < 2 * LAYERS
    east = lane < LAYERS
    top = (lane == LAYERS - 1) | (lane == 2 * LAYERS - 1)
    bottom = (lane == 0) | (lane == LAYERS)
    for s in range(OSTEPS):
        low = 2 + s
        below = now_ref[low - 1]
        here = now_ref[low]
        for r in range(low, EXT_R - low):
            above = now_ref[r + 1]
            laplace = above + below + pltpu.roll(here, EXT_C - 1, 0) + pltpu.roll(here, 1, 0) - 4.0 * here
            moving = here + drift_ref[r]
            turning = jnp.where(
                east, pltpu.roll(moving, LANES - LAYERS, 1), -pltpu.roll(moving, LAYERS, 1)
            )
            over = jnp.where(top, 0.0, pltpu.roll(here, LANES - 1, 1))
            under = jnp.where(bottom, 0.0, pltpu.roll(here, 1, 1))
            tendency = (
                viscous * laplace + turning + mixing * (over + under - 2.0 * here) - friction * here
            )
            result = jnp.where(used, (here + ocean_dt * tendency) * sea_ref[r], 0.0)
            if s == OSTEPS - 1:
                o_ref[r - HALO] = result[0:COLS]
            else:
                now_ref[r] = result
            below, here = here, above


def shape_of(*dims, dtype=f32):
    return jax.ShapeDtypeStruct(dims, dtype)


vmem = pl.BlockSpec(memory_space=pltpu.VMEM)


def call(kernel, name, operands, out_shape, scratch, mebibytes):
    return pl.pallas_call(
        kernel,
        out_shape=out_shape,
        in_specs=[vmem] * len(operands),
        out_specs=jax.tree.map(lambda _: vmem, out_shape),
        scratch_shapes=[pltpu.VMEM(shape, f32) for shape in scratch],
        compiler_params=pltpu.CompilerParams(vmem_limit_bytes=mebibytes * 2**20),
        name=name,
    )(*operands)


by_rows = pl.BlockSpec((8 * ROWS, 2 * LANES), lambda i: (i, 0))
by_chunks = pl.BlockSpec((FREQS, 8, LANES), lambda i: (0, i, 0))


def relayout(kernel, name, x, in_spec, out_spec, out_shape):
    return pl.pallas_call(
        kernel,
        grid=(pl.cdiv(DIR, 8),),
        out_shape=out_shape,
        in_specs=[in_spec],
        out_specs=out_spec,
        scratch_shapes=[pltpu.VMEM((2, 8 * ROWS, LANES), f32)],
        compiler_params=pltpu.CompilerParams(vmem_limit_bytes=4 * 2**20),
        name=name,
    )(x)


def spread(x):
    x = x.reshape(DIR * ROWS, 2 * LANES)
    return relayout(spread_kernel, "spread", x, by_rows, by_chunks, shape_of(FREQS, DIR, LANES))


def collect(x):
    out_shape = shape_of(DIR * ROWS, 2 * LANES)
    out = relayout(collect_kernel, "collect", x, by_chunks, by_rows, out_shape)
    return out.reshape(1, DIR, ROWS, 2 * LANES)


tile_shapes = [shape_of(ROWS, COLS, WIDE)] + [shape_of(ROWS, HALO, WIDE)] * 2
ext_shape = shape_of(EXT_R, EXT_C, LANES)
face_shape = shape_of(EXT_R, EXT_C, COMP)


def unpack(x, velocity):
    return call(unpack_kernel, "unpack", [x, velocity], tile_shapes, [(COMP, LANES)], 8)


def ends(*pieces):
    return call(ends_kernel, "ends", pieces, [shape_of(HALO, EXT_C, WIDE)] * 2, [], 4)


def run_cycle(first, operands):
    if first:
        out_shape = tile_shapes + [ext_shape, face_shape, face_shape]
    else:
        out_shape = [shape_of(FREQS, DIR, LANES), ext_shape]
    return call(
        lambda *refs: cycle_kernel(first, *refs),
        "cycle_first" if first else "cycle_last",
        operands,
        out_shape,
        [(EXT_R, EXT_C, LANES), (ROWS, COLS, COMP)],
        24,
    )


def ocean(velocity, stokes, sea):
    out_shape = shape_of(ROWS, COLS, LANES)
    return call(ocean_kernel, "ocean", [velocity, stokes, sea], out_shape, [(EXT_R, EXT_C, LANES)], 4)


def body(
    spectrum,
    velocity,
    gain_matrix,
    quad_matrix,
    limiter_flags,
    sea_mask,
    current_route,
    stokes_route,
):
    band_index = lax.axis_index("band")
    freq_index = lax.axis_index("freq")
    chunks = lax.all_to_all(spread(spectrum), "freq", split_axis=0, concat_axis=0, tiled=True)

    tile = jnp.transpose(velocity, (2, 3, 0, 1)).reshape(ROWS, COLS, 2 * LAYERS)
    tile = jnp.pad(tile, ((0, 0), (0, 0), (0, LANES - 2 * LAYERS)))

    cos_table, sin_table = directions(DIR)
    speeds = speed_of(jnp.arange(FREQS, dtype=jnp.int32), FREQS)
    waves = 0.5 * speeds[None, :, None] * jnp.stack([cos_table, sin_table])[:, None, :]
    waves = waves.reshape(2, 1, COMP)
    lane_ids = jnp.arange(LANES, dtype=jnp.int32)[None, :, None]
    routes = jnp.repeat(current_route, DIR)[None, None, :]
    starts = jnp.array([0, LAYERS], jnp.int32)[:, None, None]
    picker = (lane_ids == routes + starts).astype(jnp.bfloat16)
    picker = jnp.concatenate([picker] * 3, axis=1)

    def window(grid):
        padded = jnp.pad(grid, ((0, 0), (HALO, HALO), (HALO, HALO))).astype(f32)
        part = lax.dynamic_slice(
            padded,
            (0, band_index * ROWS, freq_index * COLS),
            (grid.shape[0], EXT_R, EXT_C),
        )
        part = jnp.concatenate([part[:, :, HALO:], part[:, :, :HALO]], axis=2)
        return jnp.broadcast_to(part[..., None], part.shape + (LANES,))

    flags = window(limiter_flags)
    sea = window(sea_mask[None])[0]

    numbers = wavenumber(jnp.arange(FREQS, dtype=jnp.int32), FREQS) * DIR ** (-0.5)
    deposit = deposit_table(stokes_route) * numbers[:, None]
    both = jnp.stack([cos_table, sin_table])
    weight = (both.T[None, :, :, None] * deposit[:, None, None, :]).reshape(COMP, 2 * LAYERS)
    weight = jnp.pad(weight, ((0, 0), (0, LANES - 2 * LAYERS)))
    weight_hi = lax.reduce_precision(weight, 8, 7)
    weight_lo = (weight - weight_hi).astype(jnp.bfloat16)
    weights = [weight_hi.astype(jnp.bfloat16), weight_lo]

    pieces = widen(*unpack(chunks, tile))
    results = run_cycle(
        True, [*pieces, flags[:SUB], sea, gain_matrix, quad_matrix, waves, picker, *weights]
    )
    velocity_ext, north, east = results[3:]
    pieces = widen(*results[:3])
    chunks, stokes_ext = run_cycle(
        False, [*pieces, flags[SUB:], sea, gain_matrix, quad_matrix, north, east]
    )
    chunks = lax.all_to_all(chunks, "freq", split_axis=0, concat_axis=0, tiled=True)
    ocean_out = ocean(velocity_ext, stokes_ext, sea)
    ocean_out = ocean_out[:, :, : 2 * LAYERS].reshape(ROWS, COLS, 2, LAYERS)
    velocity_out = jnp.transpose(ocean_out, (2, 3, 0, 1))
    return (collect(chunks), velocity_out)


def solution(mesh):
    return jax.shard_map(
        body,
        mesh=mesh,
        in_specs=(
            P("freq", None, "band", None),
            P(None, None, "band", "freq"),
            P(),
            P(),
            P(),
            P(),
            P(),
            P(),
        ),
        out_specs=(P("freq", None, "band", None), P(None, None, "band", "freq")),
        check_vma=False,
    )
```

```python
import jax
import jax.numpy as jnp
from jax import lax
from jax.experimental import pallas as pl
from jax.experimental.pallas import tpu as pltpu
from jax.sharding import PartitionSpec as P

DIR = 36
FREQS = 32
COMP = 1152
LAYERS = 24
SUB = 4
CYCLES = 2
OSTEPS = 3
BANDS = 8
ROWS = 16
COLS = 8
HALO = 4
EXT_R = 24
EXT_C = 16
LANES = 128
GROUPS = 9
WIDE = COMP + LANES
QUADS = COMP // 4

precise = lax.Precision.HIGHEST
ocean_dt = 0.2
viscous = 0.5
mixing = 0.5
friction = 0.1

f32 = jnp.float32


def directions(how_many):
    angles = (jnp.arange(how_many, dtype=f32) + 0.5) * (2.0 * jnp.pi / how_many)
    return (jnp.cos(angles), jnp.sin(angles))


def speed_of(position, total_count):
    return 0.5 + 0.3 * (position.astype(f32) + 0.5) / total_count


def wavenumber(position, total_count):
    return 0.5 + 1.5 * (position.astype(f32) + 0.5) / total_count


def deposit_table(stokes_route):
    layer_ids = jnp.arange(LAYERS, dtype=jnp.int32)
    weights = 1.0 / (1.0 + jnp.arange(stokes_route.shape[1], dtype=f32))
    hits = (stokes_route[:, :, None] == layer_ids[None, None, :]).astype(f32)
    return jnp.sum(hits * weights[None, :, None], axis=1)


def line(count, shift):
    return [(i, i - shift) for i in range(count) if 0 <= i - shift < count]


def widen(own, to_last, to_next):
    from_next = lax.ppermute(to_last, "freq", line(FREQS, 1))
    from_last = lax.ppermute(to_next, "freq", line(FREQS, -1))
    first, last = ends(own, from_next, from_last)
    from_up = lax.ppermute(first, "band", line(BANDS, 1))
    from_down = lax.ppermute(last, "band", line(BANDS, -1))
    return [own, from_next, from_last, from_up, from_down]


def fill(ext_ref, pieces, lanes):
    own, from_next, from_last, from_up, from_down = pieces
    middle = slice(HALO, HALO + ROWS)
    ext_ref[middle, 0:COLS, :] = own[:, :, lanes]
    ext_ref[middle, COLS : COLS + HALO, :] = from_next[:, :, lanes]
    ext_ref[middle, COLS + HALO : EXT_C, :] = from_last[:, :, lanes]
    ext_ref[HALO + ROWS : EXT_R] = from_up[:, :, lanes]
    ext_ref[0:HALO] = from_down[:, :, lanes]


def swap_blocks(tiles):
    block = lax.broadcasted_iota(jnp.int32, tiles[0].shape, 1) // 8
    for bit in (1, 2, 4, 8):
        upper = (block & bit) != 0
        fresh = list(tiles)
        for low in range(16):
            if low & bit:
                continue
            high = low | bit
            fresh[low] = jnp.where(upper, pltpu.roll(tiles[high], bit * 8, 1), tiles[low])
            fresh[high] = jnp.where(upper, tiles[high], pltpu.roll(tiles[low], LANES - bit * 8, 1))
        tiles = fresh
    return tiles


def direction_groups():
    for index in range(5):
        count = min(8, DIR - 8 * index)
        for half in range(2):
            yield index, count, half, 2 * index + half


def rows_copy(hbm_ref, vmem_ref, sems, group, outward):
    index, count, half, slot = group
    far = hbm_ref.at[pl.ds(index * 8 * ROWS, count * ROWS), pl.ds(half * LANES, LANES)]
    near = vmem_ref.at[slot, pl.ds(0, count * ROWS)]
    pair = (near, far) if outward else (far, near)
    return pltpu.make_async_copy(*pair, sems.at[slot])


def spread_kernel(x_hbm, o_hbm, half_ref, chunk_ref, in_sems, out_sems):
    copies = [rows_copy(x_hbm, half_ref, in_sems, group, False) for group in direction_groups()]
    for copy in copies:
        copy.start()
    sent = []
    for index, count, half, slot in direction_groups():
        copies[slot].wait()
        tiles = [half_ref[slot, pl.ds(r, count, stride=ROWS), :] for r in range(ROWS)]
        for i, tile in enumerate(swap_blocks(tiles)):
            for j in range(count // 4):
                chunk_ref[half * ROWS + i, 2 * index + j] = tile[4 * j : 4 * j + 4]
        if half:
            part = pl.ds(2 * index, count // 4)
            sent.append(
                pltpu.make_async_copy(chunk_ref.at[:, part], o_hbm.at[:, part], out_sems.at[index])
            )
            sent[-1].start()
    for copy in sent:
        copy.wait()


def collect_kernel(x_ref, o_hbm, half_ref, sems):
    copies = []
    for group in direction_groups():
        index, count, half, slot = group
        tiles = []
        for i in range(ROWS):
            quads = [x_ref[half * ROWS + i, 2 * index + j] for j in range(count // 4)]
            tiles.append(jnp.concatenate(quads, axis=0))
        for r, tile in enumerate(swap_blocks(tiles)):
            half_ref[slot, pl.ds(r, count, stride=ROWS), :] = tile
        copies.append(rows_copy(o_hbm, half_ref, sems, group, True))
        copies[-1].start()
    for copy in copies:
        copy.wait()


def ends_kernel(own, from_next, from_last, first_ref, last_ref):
    for ref, rows in ((first_ref, slice(0, HALO)), (last_ref, slice(ROWS - HALO, ROWS))):
        ref[:, 0:COLS, :] = own[rows]
        ref[:, COLS : COLS + HALO, :] = from_next[rows]
        ref[:, COLS + HALO : EXT_C, :] = from_last[rows]


def put(value, refs, lanes):
    refs[0][:, :, lanes] = value
    refs[1][:, :, lanes] = value[:, :HALO, :]
    refs[2][:, :, lanes] = value[:, HALO:, :]


def unpack_kernel(x_ref, u_ref, *rest):
    out_refs, flat_ref = rest[:-1], rest[-1]
    for q in range(QUADS):
        flat_ref[4 * q : 4 * q + 4, :] = x_ref[q]
    for k in range(GROUPS):
        lanes = slice(k * LANES, (k + 1) * LANES)
        put(jnp.transpose(flat_ref[lanes, :]).reshape(ROWS, COLS, LANES), out_refs, lanes)
    put(u_ref[...], out_refs, slice(COMP, WIDE))


def face_flux(lower, upper, half_courant, half_square, second):
    q = jnp.where(second, half_square, jnp.abs(half_courant))
    return lower * (half_courant + q) + upper * (half_courant - q)


def courants(ext_ref, lane_ref, pick_ref, face_refs):
    lane = lax.broadcasted_iota(jnp.int32, (EXT_C, LANES), 1)
    quarter = (0.25 * 0.15) * jnp.tanh(ext_ref[...])
    faces = []
    for r in range(EXT_R):
        along_rows = quarter[r] + quarter[min(r + 1, EXT_R - 1)]
        along_cols = quarter[r] + pltpu.roll(quarter[r], 1, 0)
        faces.append(jnp.where(lane < LAYERS, along_cols, along_rows))
    faces = jnp.concatenate(faces, axis=0)
    high = faces.astype(jnp.bfloat16).astype(f32)
    rest = faces - high
    middle = rest.astype(jnp.bfloat16).astype(f32)
    parts = jnp.concatenate([high + pltpu.roll(middle, LANES // 2, 1), rest - middle], axis=1)
    parts = parts.astype(jnp.bfloat16)
    for index in range(2):
        picked = jnp.dot(parts, pick_ref[index], preferred_element_type=f32)
        half_courant = (lane_ref[index] + picked).reshape(EXT_R, EXT_C, COMP)
        face_refs[2 * index][...] = half_courant
        face_refs[2 * index + 1][...] = (half_courant + half_courant) * half_courant


def cycle_kernel(first, *refs):
    refs = list(refs)
    take = lambda n: [refs.pop(0) for _ in range(n)]
    pieces = take(5)
    flag_ref, sea_ref, gain_ref, quad_ref = take(4)
    flag_base = 0 if first else SUB
    if first:
        lane_ref, pick_ref, weight_hi, weight_lo = take(4)
        out_refs = take(3)
        (ext_ref,) = take(1)
        face_refs = take(4)
    else:
        face_refs = take(4)
        out_hbm, ext_ref = take(2)
    tile_ref, energy_ref = take(2)
    if not first:
        chunk_ref, sems = take(2)
    fill(ext_ref, pieces, slice(COMP, WIDE))
    if first:
        courants(ext_ref, lane_ref, pick_ref, face_refs)
    east, east_square, north, north_square = face_refs
    copies = []

    def advect(k, carry):
        lanes = pl.ds(pl.multiple_of(k * LANES, LANES), LANES)
        fill(tile_ref, pieces, lanes)
        for s in range(SUB):
            here = tile_ref[s]
            above = tile_ref[s + 1]
            flag = flag_ref[flag_base + s, s + 1] != 0.0
            flux_below = face_flux(here, above, north[s, :, lanes], north_square[s, :, lanes], flag)
            for r in range(s + 1, EXT_R - 1 - s):
                here = above
                above = tile_ref[r + 1]
                flag_above = flag_ref[flag_base + s, r + 1] != 0.0
                flux_above = face_flux(
                    here, above, north[r, :, lanes], north_square[r, :, lanes], flag_above
                )
                shifted = here - (flux_above - flux_below)
                flux_east = face_flux(
                    pltpu.roll(shifted, 1, 0),
                    shifted,
                    east[r, :, lanes],
                    east_square[r, :, lanes],
                    flag,
                )
                result = shifted - (pltpu.roll(flux_east, EXT_C - 1, 0) - flux_east)
                result = result * sea_ref[r]
                if s == SUB - 1:
                    energy_ref[r - HALO, :, lanes] = result[0:COLS]
                else:
                    tile_ref[r] = result
                flux_below = flux_above
                flag = flag_above
        return carry

    lax.fori_loop(0, GROUPS, advect, 0)
    cells = ROWS * COLS
    energy = energy_ref[...].reshape(cells, COMP)
    rounded = energy.astype(jnp.bfloat16)
    squared = (energy * energy).astype(jnp.bfloat16)
    if first:
        rest = (energy - rounded.astype(f32)).astype(jnp.bfloat16)
        mm = lambda a, b: jnp.dot(a, b, preferred_element_type=f32)
        stokes = mm(rounded, weight_hi[...]) + (mm(rest, weight_hi[...]) + mm(rounded, weight_lo[...]))
        stokes = stokes.reshape(ROWS, COLS, LANES)
        put(stokes, out_refs, pl.ds(COMP, LANES))
    nt = (((1,), (1,)), ((), ()))
    for k in range(GROUPS):
        lanes = pl.ds(k * LANES, LANES)
        gain = lax.dot_general(rounded, gain_ref[lanes, :], nt, preferred_element_type=f32)
        quartic = lax.dot_general(squared, quad_ref[lanes, :], nt, preferred_element_type=f32)
        before = energy_ref[:, :, lanes].reshape(cells, LANES)
        updated = before * (1.0 + 0.5 * jnp.tanh(gain) - 0.25 * jnp.tanh(quartic))
        if first:
            put(updated.reshape(ROWS, COLS, LANES), out_refs, lanes)
        else:
            flat = jnp.transpose(updated)
            for q in range(32):
                chunk_ref[32 * k + q] = flat[4 * q : 4 * q + 4]
            part = pl.ds(32 * k, 32)
            copies.append(pltpu.make_async_copy(chunk_ref.at[part], out_hbm.at[part], sems.at[k]))
            copies[-1].start()
    for copy in copies:
        copy.wait()


def ocean_kernel(u_ref, drift_ref, sea_ref, o_ref, now_ref):
    now_ref[...] = u_ref[...]
    lane = lax.broadcasted_iota(jnp.int32, (EXT_C, LANES), 1)
    used = lane < 2 * LAYERS
    east = lane < LAYERS
    top = (lane == LAYERS - 1) | (lane == 2 * LAYERS - 1)
    bottom = (lane == 0) | (lane == LAYERS)
    for s in range(OSTEPS):
        low = 2 + s
        below = now_ref[low - 1]
        here = now_ref[low]
        for r in range(low, EXT_R - low):
            above = now_ref[r + 1]
            laplace = above + below + pltpu.roll(here, EXT_C - 1, 0) + pltpu.roll(here, 1, 0) - 4.0 * here
            moving = here + drift_ref[r]
            turning = jnp.where(
                east, pltpu.roll(moving, LANES - LAYERS, 1), -pltpu.roll(moving, LAYERS, 1)
            )
            over = jnp.where(top, 0.0, pltpu.roll(here, LANES - 1, 1))
            under = jnp.where(bottom, 0.0, pltpu.roll(here, 1, 1))
            tendency = (
                viscous * laplace + turning + mixing * (over + under - 2.0 * here) - friction * here
            )
            result = jnp.where(used, (here + ocean_dt * tendency) * sea_ref[r], 0.0)
            if s == OSTEPS - 1:
                o_ref[r - HALO] = result[0:COLS]
            else:
                now_ref[r] = result
            below, here = here, above


def shape_of(*dims, dtype=f32):
    return jax.ShapeDtypeStruct(dims, dtype)


vmem = pl.BlockSpec(memory_space=pltpu.VMEM)
hbm = pl.BlockSpec(memory_space=pltpu.HBM)


def call(kernel, name, operands, out_shape, scratch, mebibytes, in_specs=None, out_specs=None):
    return pl.pallas_call(
        kernel,
        out_shape=out_shape,
        in_specs=in_specs or [vmem] * len(operands),
        out_specs=out_specs or jax.tree.map(lambda _: vmem, out_shape),
        scratch_shapes=[pltpu.VMEM(x, f32) if isinstance(x, tuple) else x for x in scratch],
        compiler_params=pltpu.CompilerParams(vmem_limit_bytes=mebibytes * 2**20),
        name=name,
    )(*operands)


halves = (10, 8 * ROWS, LANES)
chunks_dims = (FREQS, DIR // 4, 4, LANES)
sems = pltpu.SemaphoreType.DMA


def spread(x):
    x = x.reshape(DIR * ROWS, 2 * LANES)
    scratch = [halves, chunks_dims, sems((10,)), sems((5,))]
    out = call(spread_kernel, "spread", [x], shape_of(*chunks_dims), scratch, 4, [hbm], hbm)
    return out.reshape(QUADS, 4, LANES)


def collect(x):
    out_shape = shape_of(DIR * ROWS, 2 * LANES)
    scratch = [halves, sems((10,))]
    x = x.reshape(chunks_dims)
    out = call(collect_kernel, "collect", [x], out_shape, scratch, 4, [vmem], hbm)
    return out.reshape(1, DIR, ROWS, 2 * LANES)


tile_shapes = [shape_of(ROWS, COLS, WIDE)] + [shape_of(ROWS, HALO, WIDE)] * 2
ext_shape = shape_of(EXT_R, EXT_C, LANES)
face_shape = shape_of(EXT_R, EXT_C, COMP)


def unpack(x, velocity):
    return call(unpack_kernel, "unpack", [x, velocity], tile_shapes, [(COMP, LANES)], 8)


def ends(*pieces):
    return call(ends_kernel, "ends", pieces, [shape_of(HALO, EXT_C, WIDE)] * 2, [], 4)


def run_cycle(first, operands):
    scratch = [(EXT_R, EXT_C, LANES), (ROWS, COLS, COMP)]
    if first:
        out_shape = tile_shapes + [ext_shape] + [face_shape] * 4
        out_specs = [vmem] * 8
    else:
        out_shape = [shape_of(QUADS, 4, LANES), ext_shape]
        out_specs = [hbm, vmem]
        scratch += [(QUADS, 4, LANES), sems((GROUPS,))]
    kernel = lambda *refs: cycle_kernel(first, *refs)
    name = "cycle_first" if first else "cycle_last"
    return call(kernel, name, operands, out_shape, scratch, 24, None, out_specs)


def ocean(velocity, stokes, sea):
    out_shape = shape_of(ROWS, COLS, LANES)
    return call(ocean_kernel, "ocean", [velocity, stokes, sea], out_shape, [(EXT_R, EXT_C, LANES)], 4)


def body(
    spectrum,
    velocity,
    gain_matrix,
    quad_matrix,
    limiter_flags,
    sea_mask,
    current_route,
    stokes_route,
):
    band_index = lax.axis_index("band")
    freq_index = lax.axis_index("freq")
    chunks = lax.all_to_all(spread(spectrum), "freq", split_axis=0, concat_axis=0, tiled=True)

    tile = jnp.transpose(velocity, (2, 3, 0, 1)).reshape(ROWS, COLS, 2 * LAYERS)
    tile = jnp.pad(tile, ((0, 0), (0, 0), (0, LANES - 2 * LAYERS)))

    cos_table, sin_table = directions(DIR)
    speeds = speed_of(jnp.arange(FREQS, dtype=jnp.int32), FREQS)
    waves = 0.5 * speeds[None, :, None] * jnp.stack([cos_table, sin_table])[:, None, :]
    waves = waves.reshape(2, 1, COMP)
    lane_ids = jnp.arange(LANES, dtype=jnp.int32)[None, :, None]
    routes = jnp.repeat(current_route, DIR)[None, None, :]
    starts = jnp.array([0, LAYERS], jnp.int32)[:, None, None]
    wanted = routes + starts
    high = (lane_ids == wanted) | (lane_ids == wanted + LANES // 2)
    picker = jnp.concatenate([high, lane_ids == wanted], axis=1).astype(jnp.bfloat16)

    def window(grid):
        padded = jnp.pad(grid, ((0, 0), (HALO, HALO), (HALO, HALO))).astype(f32)
        part = lax.dynamic_slice(
            padded,
            (0, band_index * ROWS, freq_index * COLS),
            (grid.shape[0], EXT_R, EXT_C),
        )
        part = jnp.concatenate([part[:, :, HALO:], part[:, :, :HALO]], axis=2)
        return jnp.broadcast_to(part[..., None], part.shape + (LANES,))

    flags = window(limiter_flags)
    sea = window(sea_mask[None])[0]

    numbers = wavenumber(jnp.arange(FREQS, dtype=jnp.int32), FREQS) * DIR ** (-0.5)
    deposit = deposit_table(stokes_route) * numbers[:, None]
    both = jnp.stack([cos_table, sin_table])
    weight = (both.T[None, :, :, None] * deposit[:, None, None, :]).reshape(COMP, 2 * LAYERS)
    weight = jnp.pad(weight, ((0, 0), (0, LANES - 2 * LAYERS)))
    weight_hi = lax.reduce_precision(weight, 8, 7)
    weight_lo = (weight - weight_hi).astype(jnp.bfloat16)
    weights = [weight_hi.astype(jnp.bfloat16), weight_lo]

    fixed = [flags, sea, gain_matrix, quad_matrix]
    pieces = widen(*unpack(chunks, tile))
    results = run_cycle(True, [*pieces, *fixed, waves, picker, *weights])
    velocity_ext, faces = results[3], results[4:]
    pieces = widen(*results[:3])
    chunks, stokes_ext = run_cycle(False, [*pieces, *fixed, *faces])
    chunks = lax.all_to_all(chunks, "freq", split_axis=0, concat_axis=0, tiled=True)
    ocean_out = ocean(velocity_ext, stokes_ext, sea)
    ocean_out = ocean_out[:, :, : 2 * LAYERS].reshape(ROWS, COLS, 2, LAYERS)
    velocity_out = jnp.transpose(ocean_out, (2, 3, 0, 1))
    return (collect(chunks), velocity_out)


def solution(mesh):
    return jax.shard_map(
        body,
        mesh=mesh,
        in_specs=(
            P("freq", None, "band", None),
            P(None, None, "band", "freq"),
            P(),
            P(),
            P(),
            P(),
            P(),
            P(),
        ),
        out_specs=(P("freq", None, "band", None), P(None, None, "band", "freq")),
        check_vma=False,
    )
```

```python
import jax
import jax.numpy as jnp
from jax import lax
from jax.experimental import pallas as pl
from jax.experimental.pallas import tpu as pltpu
from jax.sharding import PartitionSpec as P

DIR = 36
FREQS = 32
COMP = 1152
LAYERS = 24
SUB = 4
CYCLES = 2
OSTEPS = 3
BANDS = 8
ROWS = 16
COLS = 8
HALO = 4
EXT_R = 24
EXT_C = 16
LANES = 128
GROUPS = 9
QUADS = COMP // 4
KEPT = 10
MAIN = 8
CELLS = EXT_R * EXT_C

ocean_dt = 0.2
viscous = 0.5
mixing = 0.5
friction = 0.1

f32 = jnp.float32


def directions(how_many):
    angles = (jnp.arange(how_many, dtype=f32) + 0.5) * (2.0 * jnp.pi / how_many)
    return (jnp.cos(angles), jnp.sin(angles))


def speed_of(position, total_count):
    return 0.5 + 0.3 * (position.astype(f32) + 0.5) / total_count


def wavenumber(position, total_count):
    return 0.5 + 1.5 * (position.astype(f32) + 0.5) / total_count


def deposit_table(stokes_route):
    layer_ids = jnp.arange(LAYERS, dtype=jnp.int32)
    weights = 1.0 / (1.0 + jnp.arange(stokes_route.shape[1], dtype=f32))
    hits = (stokes_route[:, :, None] == layer_ids[None, None, :]).astype(f32)
    return jnp.sum(hits * weights[None, :, None], axis=1)


def line(count, shift):
    return [(i, i - shift) for i in range(count) if 0 <= i - shift < count]


def widen(own, to_last, to_next):
    from_next = lax.ppermute(to_last, "freq", line(FREQS, 1))
    from_last = lax.ppermute(to_next, "freq", line(FREQS, -1))
    first, last = ends(own, from_next, from_last)
    from_up = lax.ppermute(first, "band", line(BANDS, 1))
    from_down = lax.ppermute(last, "band", line(BANDS, -1))
    return [own, from_next, from_last, from_up, from_down]


def block(row, group, cols):
    start = (row * KEPT + group) * cols
    return slice(start, start + cols)


def fill(ext_ref, pieces, group):
    own, from_next, from_last, from_up, from_down = pieces
    for r in range(ROWS):
        ext_ref[HALO + r, 0:HALO, :] = from_last[block(r, group, HALO), :]
        ext_ref[HALO + r, HALO : HALO + COLS, :] = own[block(r, group, COLS), :]
        ext_ref[HALO + r, HALO + COLS : EXT_C, :] = from_next[block(r, group, HALO), :]
    for r in range(HALO):
        ext_ref[HALO + ROWS + r] = from_up[block(r, group, EXT_C), :]
        ext_ref[r] = from_down[block(r, group, EXT_C), :]


def fill_cells(cell_ref, pieces):
    own, from_next, from_last, from_up, from_down = pieces

    def take(ref, row, col, cols, ext_row, ext_col):
        start = (ext_row * EXT_C + ext_col) * MAIN
        cell_ref[start : start + MAIN, :] = ref[pl.ds(row * KEPT * cols + col, MAIN, stride=cols), :]

    for r in range(ROWS):
        for c in range(COLS):
            take(own, r, c, COLS, HALO + r, HALO + c)
        for c in range(HALO):
            take(from_next, r, c, HALO, HALO + r, HALO + COLS + c)
            take(from_last, r, c, HALO, HALO + r, c)
    for r in range(HALO):
        for c in range(EXT_C):
            take(from_up, r, c, EXT_C, HALO + ROWS + r, c)
            take(from_down, r, c, EXT_C, r, c)


def swap_blocks(tiles):
    block = lax.broadcasted_iota(jnp.int32, tiles[0].shape, 1) // 8
    for bit in (1, 2, 4, 8):
        upper = (block & bit) != 0
        fresh = list(tiles)
        for low in range(16):
            if low & bit:
                continue
            high = low | bit
            fresh[low] = jnp.where(upper, pltpu.roll(tiles[high], bit * 8, 1), tiles[low])
            fresh[high] = jnp.where(upper, tiles[high], pltpu.roll(tiles[low], LANES - bit * 8, 1))
        tiles = fresh
    return tiles


def direction_groups():
    for index in range(5):
        count = min(8, DIR - 8 * index)
        for half in range(2):
            yield index, count, half, 2 * index + half


def rows_copy(hbm_ref, vmem_ref, sems, group, outward):
    index, count, half, slot = group
    far = hbm_ref.at[pl.ds(index * 8 * ROWS, count * ROWS), pl.ds(half * LANES, LANES)]
    near = vmem_ref.at[slot, pl.ds(0, count * ROWS)]
    pair = (near, far) if outward else (far, near)
    return pltpu.make_async_copy(*pair, sems.at[slot])


def spread_kernel(x_hbm, o_hbm, half_ref, chunk_ref, in_sems, out_sems):
    groups = list(direction_groups())
    copies = [rows_copy(x_hbm, half_ref, in_sems, group, False) for group in groups]
    for copy in copies:
        copy.start()
    sent = []
    for batch, quads in ((groups[:6], pl.ds(0, 6)), (groups[6:], pl.ds(6, 3))):
        for group in batch:
            copies[group[3]].wait()
        for index, count, half, slot in batch:
            tiles = [half_ref[slot, pl.ds(r, count, stride=ROWS), :] for r in range(ROWS)]
            for i, tile in enumerate(swap_blocks(tiles)):
                for j in range(count // 4):
                    chunk_ref[half * ROWS + i, 2 * index + j] = tile[4 * j : 4 * j + 4]
        far = o_hbm.at[:, quads]
        sent.append(pltpu.make_async_copy(chunk_ref.at[:, quads], far, out_sems.at[len(sent)]))
        sent[-1].start()
    for copy in sent:
        copy.wait()


def collect_kernel(x_ref, o_hbm, half_ref, sems):
    groups = list(direction_groups())
    copies = []
    for batch in (groups[:6], groups[6:]):
        for index, count, half, slot in batch:
            tiles = []
            for i in range(ROWS):
                quads = [x_ref[half * ROWS + i, 2 * index + j] for j in range(count // 4)]
                tiles.append(jnp.concatenate(quads, axis=0))
            for r, tile in enumerate(swap_blocks(tiles)):
                half_ref[slot, pl.ds(r, count, stride=ROWS), :] = tile
        for group in batch:
            copies.append(rows_copy(o_hbm, half_ref, sems, group, True))
            copies[-1].start()
    for copy in copies:
        copy.wait()


def ends_kernel(own, from_next, from_last, first_ref, last_ref):
    for ref, start in ((first_ref, 0), (last_ref, ROWS - HALO)):
        for r in range(HALO):
            for k in range(KEPT):
                at = block(r, k, EXT_C).start
                ref[at : at + HALO, :] = from_last[block(start + r, k, HALO), :]
                ref[at + HALO : at + HALO + COLS, :] = own[block(start + r, k, COLS), :]
                ref[at + HALO + COLS : at + EXT_C, :] = from_next[block(start + r, k, HALO), :]


def put(value, refs, group):
    for r in range(ROWS):
        row = value[r * COLS : (r + 1) * COLS, :]
        refs[0][block(r, group, COLS), :] = row
        refs[1][block(r, group, HALO), :] = row[:HALO]
        refs[2][block(r, group, HALO), :] = row[HALO:]


def unpack_kernel(x_ref, u_ref, *rest):
    out_refs, flat_ref = rest[:-1], rest[-1]
    for q in range(QUADS):
        flat_ref[4 * q : 4 * q + 4, :] = x_ref[q]
    for k in range(GROUPS):
        put(jnp.transpose(flat_ref[k * LANES : (k + 1) * LANES, :]), out_refs, k)
    put(u_ref[...], out_refs, GROUPS)


def face_flux(lower, upper, half_courant, half_square, second):
    q = jnp.where(second, half_square, jnp.abs(half_courant))
    return lower * (half_courant + q) + upper * (half_courant - q)


def courants(ext_ref, lane_ref, pick_ref, main_ref, rest_ref):
    lane = lax.broadcasted_iota(jnp.int32, (EXT_C, LANES), 1)
    quarter = (0.25 * 0.15) * jnp.tanh(ext_ref[...])
    faces = []
    for r in range(EXT_R):
        along_rows = quarter[r] + quarter[min(r + 1, EXT_R - 1)]
        along_cols = quarter[r] + pltpu.roll(quarter[r], 1, 0)
        faces.append(jnp.where(lane < LAYERS, along_cols, along_rows))
    faces = jnp.concatenate(faces, axis=0)
    high = faces.astype(jnp.bfloat16).astype(f32)
    rest = faces - high
    middle = rest.astype(jnp.bfloat16).astype(f32)
    parts = jnp.concatenate([high + pltpu.roll(middle, LANES // 2, 1), rest - middle], axis=1)
    parts = parts.astype(jnp.bfloat16)
    for index in range(2):
        for k in range(GROUPS):
            lanes = slice(k * LANES, (k + 1) * LANES)
            picked = jnp.dot(parts, pick_ref[index, :, lanes], preferred_element_type=f32)
            half_courant = lane_ref[index, :, lanes] + picked
            square = (half_courant + half_courant) * half_courant
            for which, value in ((2 * index, half_courant), (2 * index + 1, square)):
                if k == MAIN:
                    rest_ref[which] = value.reshape(EXT_R, EXT_C, LANES)
                    continue
                for start in range(0, CELLS, 8):
                    at = (which * CELLS + start) * MAIN + k
                    main_ref[pl.ds(at, 8, stride=MAIN), :] = value[start : start + 8, :]


def advect_cells(cell_ref, face_ref, flag_ref, sea_ref, energy_ref, flag_base):
    def at(start):
        return pl.ds(start * MAIN, MAIN)

    def cell(r, c):
        return cell_ref[at(r * EXT_C + c), :]

    def flux(lower, upper, which, r, c, flag_row):
        half_courant = face_ref[at(which * CELLS + r * EXT_C + c), :]
        half_square = face_ref[at((which + 1) * CELLS + r * EXT_C + c), :]
        second = flag_ref[pl.ds(flag_row * EXT_C + c, MAIN, stride=0), :] != 0.0
        return face_flux(lower, upper, half_courant, half_square, second)

    for s in range(SUB):
        cols = range(s, EXT_C - s)
        flag_top = (flag_base + s) * EXT_R

        def upper_flux(r, c):
            return flux(cell(r, c), cell(r + 1, c), 2, r, c, flag_top + r + 1)

        def row(r, below):
            above = [upper_flux(r, c) for c in cols]
            shifted = [cell(r, c) - (a - b) for c, a, b in zip(cols, above, below)]
            along = [
                flux(shifted[i - 1], shifted[i], 0, r, cols[i], flag_top + r)
                for i in range(1, len(cols))
            ]
            for i in range(1, len(cols) - 1):
                sea = sea_ref[pl.ds(r * EXT_C + cols[i], MAIN, stride=0), :]
                result = (shifted[i] - (along[i] - along[i - 1])) * sea
                if s == SUB - 1:
                    start = (r - HALO) * GROUPS * COLS + cols[i] - HALO
                    energy_ref[pl.ds(start, MAIN, stride=COLS), :] = result
                else:
                    cell_ref[at(r * EXT_C + cols[i]), :] = result
            return above

        below = [upper_flux(s, c) for c in cols]
        for r in range(s + 1, EXT_R - 1 - s):
            below = row(r, below)


def advect_rest(tile_ref, face_ref, flag_ref, sea_ref, energy_ref, flag_base):
    def rows_of(ref, r):
        return ref[r * EXT_C : (r + 1) * EXT_C, :]

    for s in range(SUB):
        flag_top = (flag_base + s) * EXT_R
        here = tile_ref[s]
        above = tile_ref[s + 1]
        flag = rows_of(flag_ref, flag_top + s + 1) != 0.0
        flux_below = face_flux(here, above, face_ref[2, s], face_ref[3, s], flag)
        for r in range(s + 1, EXT_R - 1 - s):
            here = above
            above = tile_ref[r + 1]
            flag_above = rows_of(flag_ref, flag_top + r + 1) != 0.0
            flux_above = face_flux(here, above, face_ref[2, r], face_ref[3, r], flag_above)
            shifted = here - (flux_above - flux_below)
            flux_east = face_flux(
                pltpu.roll(shifted, 1, 0), shifted, face_ref[0, r], face_ref[1, r], flag
            )
            result = shifted - (pltpu.roll(flux_east, EXT_C - 1, 0) - flux_east)
            result = result * rows_of(sea_ref, r)
            if s == SUB - 1:
                start = ((r - HALO) * GROUPS + MAIN) * COLS
                energy_ref[start : start + COLS, :] = result[HALO : HALO + COLS]
            else:
                tile_ref[r] = result
            flux_below = flux_above
            flag = flag_above


def cycle_kernel(first, *refs):
    refs = list(refs)
    take = lambda n: [refs.pop(0) for _ in range(n)]
    pieces = take(5)
    flag_ref, sea_ref, gain_ref, quad_ref = take(4)
    flag_base = 0 if first else SUB
    if first:
        lane_ref, pick_ref, weight_hi, weight_lo = take(4)
        out_refs = take(3)
        (ext_ref,) = take(1)
        main_ref, rest_ref = take(2)
    else:
        main_ref, rest_ref = take(2)
        out_hbm, ext_ref = take(2)
    cell_ref, tile_ref, energy_ref = take(3)
    if not first:
        chunk_ref, sems = take(2)
    fill(ext_ref, pieces, GROUPS)
    if first:
        courants(ext_ref, lane_ref, pick_ref, main_ref, rest_ref)
    fill_cells(cell_ref, pieces)
    fill(tile_ref, pieces, MAIN)
    advect_rest(tile_ref, rest_ref, flag_ref, sea_ref, energy_ref, flag_base)
    advect_cells(cell_ref, main_ref, flag_ref, sea_ref, energy_ref, flag_base)

    def energy_group(k):
        starts = [(r * GROUPS + k) * COLS for r in range(ROWS)]
        return jnp.concatenate([energy_ref[a : a + COLS, :] for a in starts], axis=0)

    copies = []
    energy = jnp.concatenate([energy_group(k) for k in range(GROUPS)], axis=1)
    rounded = energy.astype(jnp.bfloat16)
    squared = (energy * energy).astype(jnp.bfloat16)
    if first:
        rest = (energy - rounded.astype(f32)).astype(jnp.bfloat16)
        mm = lambda a, b: jnp.dot(a, b, preferred_element_type=f32)
        stokes = mm(rounded, weight_hi[...]) + (mm(rest, weight_hi[...]) + mm(rounded, weight_lo[...]))
        put(stokes, out_refs, GROUPS)
    nt = (((1,), (1,)), ((), ()))
    for k in range(GROUPS):
        lanes = pl.ds(k * LANES, LANES)
        gain = lax.dot_general(rounded, gain_ref[lanes, :], nt, preferred_element_type=f32)
        quartic = lax.dot_general(squared, quad_ref[lanes, :], nt, preferred_element_type=f32)
        updated = energy_group(k) * (1.0 + 0.5 * jnp.tanh(gain) - 0.25 * jnp.tanh(quartic))
        if first:
            put(updated, out_refs, k)
        else:
            flat = jnp.transpose(updated)
            for q in range(32):
                chunk_ref[32 * k + q] = flat[4 * q : 4 * q + 4]
            part = pl.ds(32 * k, 32)
            copies.append(pltpu.make_async_copy(chunk_ref.at[part], out_hbm.at[part], sems.at[k]))
            copies[-1].start()
    for copy in copies:
        copy.wait()


def ocean_kernel(u_ref, drift_ref, sea_ref, o_ref, now_ref):
    now_ref[...] = u_ref[...]
    lane = lax.broadcasted_iota(jnp.int32, (EXT_C, LANES), 1)
    used = lane < 2 * LAYERS
    east = lane < LAYERS
    top = (lane == LAYERS - 1) | (lane == 2 * LAYERS - 1)
    bottom = (lane == 0) | (lane == LAYERS)
    for s in range(OSTEPS):
        low = 2 + s
        below = now_ref[low - 1]
        here = now_ref[low]
        for r in range(low, EXT_R - low):
            above = now_ref[r + 1]
            laplace = above + below + pltpu.roll(here, EXT_C - 1, 0) + pltpu.roll(here, 1, 0) - 4.0 * here
            moving = here + drift_ref[r]
            turning = jnp.where(
                east, pltpu.roll(moving, LANES - LAYERS, 1), -pltpu.roll(moving, LAYERS, 1)
            )
            over = jnp.where(top, 0.0, pltpu.roll(here, LANES - 1, 1))
            under = jnp.where(bottom, 0.0, pltpu.roll(here, 1, 1))
            tendency = (
                viscous * laplace + turning + mixing * (over + under - 2.0 * here) - friction * here
            )
            result = jnp.where(used, (here + ocean_dt * tendency) * sea_ref[r * EXT_C : (r + 1) * EXT_C, :], 0.0)
            if s == OSTEPS - 1:
                o_ref[r - HALO] = result[HALO : HALO + COLS]
            else:
                now_ref[r] = result
            below, here = here, above


def shape_of(*dims, dtype=f32):
    return jax.ShapeDtypeStruct(dims, dtype)


vmem = pl.BlockSpec(memory_space=pltpu.VMEM)
hbm = pl.BlockSpec(memory_space=pltpu.HBM)


def call(kernel, name, operands, out_shape, scratch, mebibytes, in_specs=None, out_specs=None):
    return pl.pallas_call(
        kernel,
        out_shape=out_shape,
        in_specs=in_specs or [vmem] * len(operands),
        out_specs=out_specs or jax.tree.map(lambda _: vmem, out_shape),
        scratch_shapes=[pltpu.VMEM(x, f32) if isinstance(x, tuple) else x for x in scratch],
        compiler_params=pltpu.CompilerParams(vmem_limit_bytes=mebibytes * 2**20),
        name=name,
    )(*operands)


halves = (10, 8 * ROWS, LANES)
chunks_dims = (FREQS, DIR // 4, 4, LANES)
sems = pltpu.SemaphoreType.DMA


def spread(x):
    x = x.reshape(DIR * ROWS, 2 * LANES)
    scratch = [halves, chunks_dims, sems((10,)), sems((2,))]
    out = call(spread_kernel, "spread", [x], shape_of(*chunks_dims), scratch, 4, [hbm], hbm)
    return out.reshape(QUADS, 4, LANES)


def collect(x):
    out_shape = shape_of(DIR * ROWS, 2 * LANES)
    scratch = [halves, sems((10,))]
    x = x.reshape(chunks_dims)
    out = call(collect_kernel, "collect", [x], out_shape, scratch, 4, [vmem], hbm)
    return out.reshape(1, DIR, ROWS, 2 * LANES)


tile_shapes = [shape_of(ROWS * KEPT * COLS, LANES)] + [shape_of(ROWS * KEPT * HALO, LANES)] * 2
ext_shape = shape_of(EXT_R, EXT_C, LANES)


def unpack(x, velocity):
    return call(unpack_kernel, "unpack", [x, velocity], tile_shapes, [(COMP, LANES)], 8)


def ends(*pieces):
    return call(ends_kernel, "ends", pieces, [shape_of(HALO * KEPT * EXT_C, LANES)] * 2, [], 4)


def run_cycle(first, operands):
    scratch = [(CELLS * MAIN, LANES), (EXT_R, EXT_C, LANES), (ROWS * GROUPS * COLS, LANES)]
    if first:
        faces = [shape_of(4 * CELLS * MAIN, LANES), shape_of(4, EXT_R, EXT_C, LANES)]
        out_shape = tile_shapes + [ext_shape] + faces
        out_specs = [vmem] * 6
    else:
        out_shape = [shape_of(QUADS, 4, LANES), ext_shape]
        out_specs = [hbm, vmem]
        scratch += [(QUADS, 4, LANES), sems((GROUPS,))]
    kernel = lambda *refs: cycle_kernel(first, *refs)
    name = "cycle_first" if first else "cycle_last"
    return call(kernel, name, operands, out_shape, scratch, 20, None, out_specs)


def ocean(velocity, stokes, sea):
    out_shape = shape_of(ROWS, COLS, LANES)
    return call(ocean_kernel, "ocean", [velocity, stokes, sea], out_shape, [(EXT_R, EXT_C, LANES)], 4)


def body(
    spectrum,
    velocity,
    gain_matrix,
    quad_matrix,
    limiter_flags,
    sea_mask,
    current_route,
    stokes_route,
):
    band_index = lax.axis_index("band")
    freq_index = lax.axis_index("freq")
    chunks = lax.all_to_all(spread(spectrum), "freq", split_axis=0, concat_axis=0, tiled=True)

    tile = jnp.transpose(velocity, (2, 3, 0, 1)).reshape(ROWS, COLS, 2 * LAYERS)
    tile = jnp.pad(tile, ((0, 0), (0, 0), (0, LANES - 2 * LAYERS))).reshape(ROWS * COLS, LANES)

    cos_table, sin_table = directions(DIR)
    speeds = speed_of(jnp.arange(FREQS, dtype=jnp.int32), FREQS)
    waves = 0.5 * speeds[None, :, None] * jnp.stack([cos_table, sin_table])[:, None, :]
    waves = waves.reshape(2, 1, COMP)
    lane_ids = jnp.arange(LANES, dtype=jnp.int32)[None, :, None]
    routes = jnp.repeat(current_route, DIR)[None, None, :]
    starts = jnp.array([0, LAYERS], jnp.int32)[:, None, None]
    wanted = routes + starts
    high = (lane_ids == wanted) | (lane_ids == wanted + LANES // 2)
    picker = jnp.concatenate([high, lane_ids == wanted], axis=1).astype(jnp.bfloat16)

    def window(grid):
        padded = jnp.pad(grid, ((0, 0), (HALO, HALO), (HALO, HALO))).astype(f32)
        part = lax.dynamic_slice(
            padded,
            (0, band_index * ROWS, freq_index * COLS),
            (grid.shape[0], EXT_R, EXT_C),
        )
        return jnp.broadcast_to(part[..., None], part.shape + (LANES,)).reshape(-1, LANES)

    flags = window(limiter_flags)
    sea = window(sea_mask[None])

    numbers = wavenumber(jnp.arange(FREQS, dtype=jnp.int32), FREQS) * DIR ** (-0.5)
    deposit = deposit_table(stokes_route) * numbers[:, None]
    both = jnp.stack([cos_table, sin_table])
    weight = (both.T[None, :, :, None] * deposit[:, None, None, :]).reshape(COMP, 2 * LAYERS)
    weight = jnp.pad(weight, ((0, 0), (0, LANES - 2 * LAYERS)))
    weight_hi = lax.reduce_precision(weight, 8, 7)
    weight_lo = (weight - weight_hi).astype(jnp.bfloat16)
    weights = [weight_hi.astype(jnp.bfloat16), weight_lo]

    chunks, tile, flags, sea, waves, picker, weights = lax.optimization_barrier(
        (chunks, tile, flags, sea, waves, picker, weights)
    )
    fixed = [flags, sea, gain_matrix, quad_matrix]
    pieces = widen(*unpack(chunks, tile))
    results = run_cycle(True, [*pieces, *fixed, waves, picker, *weights])
    velocity_ext, faces = results[3], results[4:]
    pieces = widen(*results[:3])
    chunks, stokes_ext = run_cycle(False, [*pieces, *fixed, *faces])
    chunks = lax.all_to_all(chunks, "freq", split_axis=0, concat_axis=0, tiled=True)
    ocean_out = ocean(velocity_ext, stokes_ext, sea)
    ocean_out = ocean_out[:, :, : 2 * LAYERS].reshape(ROWS, COLS, 2, LAYERS)
    velocity_out = jnp.transpose(ocean_out, (2, 3, 0, 1))
    return (collect(chunks), velocity_out)


def solution(mesh):
    return jax.shard_map(
        body,
        mesh=mesh,
        in_specs=(
            P("freq", None, "band", None),
            P(None, None, "band", "freq"),
            P(),
            P(),
            P(),
            P(),
            P(),
            P(),
        ),
        out_specs=(P("freq", None, "band", None), P(None, None, "band", "freq")),
        check_vma=False,
    )
```

```python
import jax
import jax.numpy as jnp
from jax import lax
from jax.experimental import pallas as pl
from jax.experimental.pallas import tpu as pltpu
from jax.sharding import PartitionSpec as P

DIR = 36
FREQS = 32
COMP = 1152
LAYERS = 24
SUB = 4
CYCLES = 2
OSTEPS = 3
BANDS = 8
ROWS = 16
COLS = 8
HALO = 4
EXT_R = 24
EXT_C = 16
LANES = 128
GROUPS = 9
QUADS = COMP // 4
KEPT = 10
MAIN = 8
CELLS = EXT_R * EXT_C

ocean_dt = 0.2
viscous = 0.5
mixing = 0.5
friction = 0.1

f32 = jnp.float32


def directions(how_many):
    angles = (jnp.arange(how_many, dtype=f32) + 0.5) * (2.0 * jnp.pi / how_many)
    return (jnp.cos(angles), jnp.sin(angles))


def speed_of(position, total_count):
    return 0.5 + 0.3 * (position.astype(f32) + 0.5) / total_count


def wavenumber(position, total_count):
    return 0.5 + 1.5 * (position.astype(f32) + 0.5) / total_count


def deposit_table(stokes_route):
    layer_ids = jnp.arange(LAYERS, dtype=jnp.int32)
    weights = 1.0 / (1.0 + jnp.arange(stokes_route.shape[1], dtype=f32))
    hits = (stokes_route[:, :, None] == layer_ids[None, None, :]).astype(f32)
    return jnp.sum(hits * weights[None, :, None], axis=1)


def line(count, shift):
    return [(i, i - shift) for i in range(count) if 0 <= i - shift < count]


def widen(own, to_last, to_next):
    from_next = lax.ppermute(to_last, "freq", line(FREQS, 1))
    from_last = lax.ppermute(to_next, "freq", line(FREQS, -1))
    first, last = ends(own, from_next, from_last)
    from_up = lax.ppermute(first, "band", line(BANDS, 1))
    from_down = lax.ppermute(last, "band", line(BANDS, -1))
    return [own, from_next, from_last, from_up, from_down]


def block(row, group, cols):
    start = (row * KEPT + group) * cols
    return slice(start, start + cols)


def fill(ext_ref, pieces, group):
    own, from_next, from_last, from_up, from_down = pieces
    for r in range(ROWS):
        ext_ref[HALO + r, 0:HALO, :] = from_last[block(r, group, HALO), :]
        ext_ref[HALO + r, HALO : HALO + COLS, :] = own[block(r, group, COLS), :]
        ext_ref[HALO + r, HALO + COLS : EXT_C, :] = from_next[block(r, group, HALO), :]
    for r in range(HALO):
        ext_ref[HALO + ROWS + r] = from_up[block(r, group, EXT_C), :]
        ext_ref[r] = from_down[block(r, group, EXT_C), :]


def fill_cells(cell_ref, pieces):
    own, from_next, from_last, from_up, from_down = pieces

    def take(ref, row, col, cols, ext_row, ext_col):
        start = (ext_row * EXT_C + ext_col) * MAIN
        cell_ref[start : start + MAIN, :] = ref[pl.ds(row * KEPT * cols + col, MAIN, stride=cols), :]

    for r in range(ROWS):
        for c in range(COLS):
            take(own, r, c, COLS, HALO + r, HALO + c)
        for c in range(HALO):
            take(from_next, r, c, HALO, HALO + r, HALO + COLS + c)
            take(from_last, r, c, HALO, HALO + r, c)
    for r in range(HALO):
        for c in range(EXT_C):
            take(from_up, r, c, EXT_C, HALO + ROWS + r, c)
            take(from_down, r, c, EXT_C, r, c)


def swap_blocks(tiles):
    block = lax.broadcasted_iota(jnp.int32, tiles[0].shape, 1) // 8
    for bit in (1, 2, 4, 8):
        upper = (block & bit) != 0
        fresh = list(tiles)
        for low in range(16):
            if low & bit:
                continue
            high = low | bit
            fresh[low] = jnp.where(upper, pltpu.roll(tiles[high], bit * 8, 1), tiles[low])
            fresh[high] = jnp.where(upper, tiles[high], pltpu.roll(tiles[low], LANES - bit * 8, 1))
        tiles = fresh
    return tiles


def direction_groups():
    for index in range(5):
        count = min(8, DIR - 8 * index)
        for half in range(2):
            yield index, count, half, 2 * index + half


def rows_copy(hbm_ref, vmem_ref, sems, group, outward):
    index, count, half, slot = group
    far = hbm_ref.at[pl.ds(index * 8 * ROWS, count * ROWS), pl.ds(half * LANES, LANES)]
    near = vmem_ref.at[slot, pl.ds(0, count * ROWS)]
    pair = (near, far) if outward else (far, near)
    return pltpu.make_async_copy(*pair, sems.at[slot])


def spread_kernel(x_hbm, o_hbm, half_ref, chunk_ref, in_sems, out_sems):
    groups = list(direction_groups())
    copies = [rows_copy(x_hbm, half_ref, in_sems, group, False) for group in groups]
    for copy in copies:
        copy.start()
    sent = []
    for batch, quads in ((groups[:6], pl.ds(0, 6)), (groups[6:], pl.ds(6, 3))):
        for group in batch:
            copies[group[3]].wait()
        for index, count, half, slot in batch:
            tiles = [half_ref[slot, pl.ds(r, count, stride=ROWS), :] for r in range(ROWS)]
            for i, tile in enumerate(swap_blocks(tiles)):
                for j in range(count // 4):
                    chunk_ref[half * ROWS + i, 2 * index + j] = tile[4 * j : 4 * j + 4]
        far = o_hbm.at[:, quads]
        sent.append(pltpu.make_async_copy(chunk_ref.at[:, quads], far, out_sems.at[len(sent)]))
        sent[-1].start()
    for copy in sent:
        copy.wait()


def collect_kernel(x_ref, o_hbm, half_ref, sems):
    groups = list(direction_groups())
    copies = []
    for batch in (groups[:6], groups[6:]):
        for index, count, half, slot in batch:
            tiles = []
            for i in range(ROWS):
                quads = [x_ref[half * ROWS + i, 2 * index + j] for j in range(count // 4)]
                tiles.append(jnp.concatenate(quads, axis=0))
            for r, tile in enumerate(swap_blocks(tiles)):
                half_ref[slot, pl.ds(r, count, stride=ROWS), :] = tile
        for group in batch:
            copies.append(rows_copy(o_hbm, half_ref, sems, group, True))
            copies[-1].start()
    for copy in copies:
        copy.wait()


def ends_kernel(own, from_next, from_last, first_ref, last_ref):
    for ref, start in ((first_ref, 0), (last_ref, ROWS - HALO)):
        for r in range(HALO):
            for k in range(KEPT):
                at = block(r, k, EXT_C).start
                ref[at : at + HALO, :] = from_last[block(start + r, k, HALO), :]
                ref[at + HALO : at + HALO + COLS, :] = own[block(start + r, k, COLS), :]
                ref[at + HALO + COLS : at + EXT_C, :] = from_next[block(start + r, k, HALO), :]


def put(value, refs, group):
    for r in range(ROWS):
        row = value[r * COLS : (r + 1) * COLS, :]
        refs[0][block(r, group, COLS), :] = row
        refs[1][block(r, group, HALO), :] = row[:HALO]
        refs[2][block(r, group, HALO), :] = row[HALO:]


def unpack_kernel(x_ref, u_ref, *rest):
    out_refs, flat_ref = rest[:-1], rest[-1]
    for q in range(QUADS):
        flat_ref[4 * q : 4 * q + 4, :] = x_ref[q]
    for k in range(GROUPS):
        put(jnp.transpose(flat_ref[k * LANES : (k + 1) * LANES, :]), out_refs, k)
    put(u_ref[...], out_refs, GROUPS)


def face_flux(lower, upper, half_courant, half_square, second):
    q = jnp.where(second, half_square, jnp.abs(half_courant))
    return lower * (half_courant + q) + upper * (half_courant - q)


def courants(ext_ref, lane_ref, main_ref, rest_ref):
    lane = lax.broadcasted_iota(jnp.int32, (EXT_C, LANES), 1)
    quarter = (0.25 * 0.15) * jnp.tanh(ext_ref[...])
    faces = []
    for r in range(EXT_R):
        along_rows = quarter[r] + quarter[min(r + 1, EXT_R - 1)]
        along_cols = quarter[r] + pltpu.roll(quarter[r], 1, 0)
        faces.append(jnp.where(lane < LAYERS, along_cols, along_rows))
    faces = jnp.concatenate(faces, axis=0)
    high = faces.astype(jnp.bfloat16).astype(f32)
    rest = faces - high
    middle = rest.astype(jnp.bfloat16).astype(f32)
    parts = jnp.concatenate([high + pltpu.roll(middle, LANES // 2, 1), rest - middle], axis=1)
    parts = parts.astype(jnp.bfloat16)
    layer = lax.broadcasted_iota(jnp.int32, (2 * LAYERS, LANES), 0).astype(f32)
    blank = jnp.zeros((LANES, LANES), f32)
    short, long = blank[: LANES // 2 - 2 * LAYERS], blank[: LANES - 2 * LAYERS]
    for index in range(2):
        for k in range(GROUPS):
            lanes = slice(k * LANES, (k + 1) * LANES)
            hit = jnp.where(layer == lane_ref[2, :, lanes] + LAYERS * index, 1.0, 0.0)
            picker = jnp.concatenate([hit, short, hit, short, hit, long], axis=0)
            picked = jnp.dot(parts, picker.astype(jnp.bfloat16), preferred_element_type=f32)
            half_courant = lane_ref[index, :, lanes] + picked
            square = (half_courant + half_courant) * half_courant
            for which, value in ((2 * index, half_courant), (2 * index + 1, square)):
                if k == MAIN:
                    rest_ref[which] = value.reshape(EXT_R, EXT_C, LANES)
                    continue
                for start in range(0, CELLS, 8):
                    at = (which * CELLS + start) * MAIN + k
                    main_ref[pl.ds(at, 8, stride=MAIN), :] = value[start : start + 8, :]


def advect_cells(cell_ref, face_ref, flag_ref, sea_ref, energy_ref, flag_base):
    def at(start):
        return pl.ds(start * MAIN, MAIN)

    def cell(r, c):
        return cell_ref[at(r * EXT_C + c), :]

    def flux(lower, upper, which, r, c, flag_row):
        half_courant = face_ref[at(which * CELLS + r * EXT_C + c), :]
        half_square = face_ref[at((which + 1) * CELLS + r * EXT_C + c), :]
        second = flag_ref[pl.ds(flag_row * EXT_C + c, MAIN, stride=0), :] != 0.0
        return face_flux(lower, upper, half_courant, half_square, second)

    for s in range(SUB):
        cols = range(s, EXT_C - s)
        flag_top = (flag_base + s) * EXT_R

        def upper_flux(r, c):
            return flux(cell(r, c), cell(r + 1, c), 2, r, c, flag_top + r + 1)

        def row(r, below):
            above = [upper_flux(r, c) for c in cols]
            shifted = [cell(r, c) - (a - b) for c, a, b in zip(cols, above, below)]
            along = [
                flux(shifted[i - 1], shifted[i], 0, r, cols[i], flag_top + r)
                for i in range(1, len(cols))
            ]
            for i in range(1, len(cols) - 1):
                sea = sea_ref[pl.ds(r * EXT_C + cols[i], MAIN, stride=0), :]
                result = (shifted[i] - (along[i] - along[i - 1])) * sea
                if s == SUB - 1:
                    start = (r - HALO) * GROUPS * COLS + cols[i] - HALO
                    energy_ref[pl.ds(start, MAIN, stride=COLS), :] = result
                else:
                    cell_ref[at(r * EXT_C + cols[i]), :] = result
            return above

        below = [upper_flux(s, c) for c in cols]
        for r in range(s + 1, EXT_R - 1 - s):
            below = row(r, below)


def advect_rest(tile_ref, face_ref, flag_ref, sea_ref, energy_ref, flag_base):
    def rows_of(ref, r):
        return ref[r * EXT_C : (r + 1) * EXT_C, :]

    for s in range(SUB):
        flag_top = (flag_base + s) * EXT_R
        here = tile_ref[s]
        above = tile_ref[s + 1]
        flag = rows_of(flag_ref, flag_top + s + 1) != 0.0
        flux_below = face_flux(here, above, face_ref[2, s], face_ref[3, s], flag)
        for r in range(s + 1, EXT_R - 1 - s):
            here = above
            above = tile_ref[r + 1]
            flag_above = rows_of(flag_ref, flag_top + r + 1) != 0.0
            flux_above = face_flux(here, above, face_ref[2, r], face_ref[3, r], flag_above)
            shifted = here - (flux_above - flux_below)
            flux_east = face_flux(
                pltpu.roll(shifted, 1, 0), shifted, face_ref[0, r], face_ref[1, r], flag
            )
            result = shifted - (pltpu.roll(flux_east, EXT_C - 1, 0) - flux_east)
            result = result * rows_of(sea_ref, r)
            if s == SUB - 1:
                start = ((r - HALO) * GROUPS + MAIN) * COLS
                energy_ref[start : start + COLS, :] = result[HALO : HALO + COLS]
            else:
                tile_ref[r] = result
            flux_below = flux_above
            flag = flag_above


def stokes_weights(angle_ref, deposit_ref, weight_ref):
    for g in range(FREQS):
        rows = angle_ref[...] * deposit_ref[g : g + 1, :]
        for d in range(0, DIR, 4):
            weight_ref[g * DIR + d : g * DIR + d + 4, :] = rows[d : d + 4]


def cycle_kernel(first, *refs):
    refs = list(refs)
    take = lambda n: [refs.pop(0) for _ in range(n)]
    pieces = take(5)
    flag_ref, sea_ref, gain_ref, quad_ref = take(4)
    flag_base = 0 if first else SUB
    if first:
        lane_ref, angle_ref, deposit_ref = take(3)
        out_refs = take(3)
        (ext_ref,) = take(1)
        main_ref, rest_ref = take(2)
    else:
        main_ref, rest_ref = take(2)
        out_hbm, ext_ref = take(2)
    cell_ref, tile_ref, energy_ref = take(3)
    if first:
        (weight_ref,) = take(1)
        stokes_weights(angle_ref, deposit_ref, weight_ref)
    else:
        chunk_ref, sems = take(2)
    fill(ext_ref, pieces, GROUPS)
    if first:
        courants(ext_ref, lane_ref, main_ref, rest_ref)
    fill_cells(cell_ref, pieces)
    fill(tile_ref, pieces, MAIN)
    advect_rest(tile_ref, rest_ref, flag_ref, sea_ref, energy_ref, flag_base)
    advect_cells(cell_ref, main_ref, flag_ref, sea_ref, energy_ref, flag_base)

    def energy_group(k):
        starts = [(r * GROUPS + k) * COLS for r in range(ROWS)]
        return jnp.concatenate([energy_ref[a : a + COLS, :] for a in starts], axis=0)

    copies = []
    energy = jnp.concatenate([energy_group(k) for k in range(GROUPS)], axis=1)
    rounded = energy.astype(jnp.bfloat16)
    squared = (energy * energy).astype(jnp.bfloat16)
    if first:
        rest = (energy - rounded.astype(f32)).astype(jnp.bfloat16)
        mm = lambda a, b: jnp.dot(a, b, preferred_element_type=f32)
        weight = weight_ref[...]
        weight_hi = weight.astype(jnp.bfloat16)
        weight_lo = (weight - weight_hi.astype(f32)).astype(jnp.bfloat16)
        stokes = mm(rounded, weight_hi) + (mm(rest, weight_hi) + mm(rounded, weight_lo))
        put(stokes, out_refs, GROUPS)
    nt = (((1,), (1,)), ((), ()))
    for k in range(GROUPS):
        lanes = pl.ds(k * LANES, LANES)
        gain = lax.dot_general(rounded, gain_ref[lanes, :], nt, preferred_element_type=f32)
        quartic = lax.dot_general(squared, quad_ref[lanes, :], nt, preferred_element_type=f32)
        updated = energy_group(k) * (1.0 + 0.5 * jnp.tanh(gain) - 0.25 * jnp.tanh(quartic))
        if first:
            put(updated, out_refs, k)
        else:
            flat = jnp.transpose(updated)
            for q in range(32):
                chunk_ref[32 * k + q] = flat[4 * q : 4 * q + 4]
            part = pl.ds(32 * k, 32)
            copies.append(pltpu.make_async_copy(chunk_ref.at[part], out_hbm.at[part], sems.at[k]))
            copies[-1].start()
    for copy in copies:
        copy.wait()


def ocean_kernel(u_ref, drift_ref, sea_ref, o_ref, now_ref):
    now_ref[...] = u_ref[...]
    lane = lax.broadcasted_iota(jnp.int32, (EXT_C, LANES), 1)
    used = lane < 2 * LAYERS
    east = lane < LAYERS
    top = (lane == LAYERS - 1) | (lane == 2 * LAYERS - 1)
    bottom = (lane == 0) | (lane == LAYERS)
    for s in range(OSTEPS):
        low = 2 + s
        below = now_ref[low - 1]
        here = now_ref[low]
        for r in range(low, EXT_R - low):
            above = now_ref[r + 1]
            laplace = above + below + pltpu.roll(here, EXT_C - 1, 0) + pltpu.roll(here, 1, 0) - 4.0 * here
            moving = here + drift_ref[r]
            turning = jnp.where(
                east, pltpu.roll(moving, LANES - LAYERS, 1), -pltpu.roll(moving, LAYERS, 1)
            )
            over = jnp.where(top, 0.0, pltpu.roll(here, LANES - 1, 1))
            under = jnp.where(bottom, 0.0, pltpu.roll(here, 1, 1))
            tendency = (
                viscous * laplace + turning + mixing * (over + under - 2.0 * here) - friction * here
            )
            result = jnp.where(used, (here + ocean_dt * tendency) * sea_ref[r * EXT_C : (r + 1) * EXT_C, :], 0.0)
            if s == OSTEPS - 1:
                o_ref[r - HALO] = result[HALO : HALO + COLS]
            else:
                now_ref[r] = result
            below, here = here, above


def shape_of(*dims, dtype=f32):
    return jax.ShapeDtypeStruct(dims, dtype)


vmem = pl.BlockSpec(memory_space=pltpu.VMEM)
hbm = pl.BlockSpec(memory_space=pltpu.HBM)


def call(kernel, name, operands, out_shape, scratch, mebibytes, in_specs=None, out_specs=None):
    return pl.pallas_call(
        kernel,
        out_shape=out_shape,
        in_specs=in_specs or [vmem] * len(operands),
        out_specs=out_specs or jax.tree.map(lambda _: vmem, out_shape),
        scratch_shapes=[pltpu.VMEM(x, f32) if isinstance(x, tuple) else x for x in scratch],
        compiler_params=pltpu.CompilerParams(vmem_limit_bytes=mebibytes * 2**20),
        name=name,
    )(*operands)


halves = (10, 8 * ROWS, LANES)
chunks_dims = (FREQS, DIR // 4, 4, LANES)
sems = pltpu.SemaphoreType.DMA


def spread(x):
    x = x.reshape(DIR * ROWS, 2 * LANES)
    scratch = [halves, chunks_dims, sems((10,)), sems((2,))]
    out = call(spread_kernel, "spread", [x], shape_of(*chunks_dims), scratch, 60, [hbm], hbm)
    return out.reshape(QUADS, 4, LANES)


def collect(x):
    out_shape = shape_of(DIR * ROWS, 2 * LANES)
    scratch = [halves, sems((10,))]
    x = x.reshape(chunks_dims)
    out = call(collect_kernel, "collect", [x], out_shape, scratch, 4, [vmem], hbm)
    return out.reshape(1, DIR, ROWS, 2 * LANES)


tile_shapes = [shape_of(ROWS * KEPT * COLS, LANES)] + [shape_of(ROWS * KEPT * HALO, LANES)] * 2
ext_shape = shape_of(EXT_R, EXT_C, LANES)


def unpack(x, velocity):
    return call(unpack_kernel, "unpack", [x, velocity], tile_shapes, [(COMP, LANES)], 8)


def ends(*pieces):
    return call(ends_kernel, "ends", pieces, [shape_of(HALO * KEPT * EXT_C, LANES)] * 2, [], 4)


def run_cycle(first, operands):
    scratch = [(CELLS * MAIN, LANES), (EXT_R, EXT_C, LANES), (ROWS * GROUPS * COLS, LANES)]
    if first:
        faces = [shape_of(4 * CELLS * MAIN, LANES), shape_of(4, EXT_R, EXT_C, LANES)]
        out_shape = tile_shapes + [ext_shape] + faces
        scratch += [(COMP, LANES)]
        out_specs = [vmem] * 6
    else:
        out_shape = [shape_of(QUADS, 4, LANES), ext_shape]
        out_specs = [hbm, vmem]
        scratch += [(QUADS, 4, LANES), sems((GROUPS,))]
    kernel = lambda *refs: cycle_kernel(first, *refs)
    name = "cycle_first" if first else "cycle_last"
    return call(kernel, name, operands, out_shape, scratch, 20, None, out_specs)


def ocean(velocity, stokes, sea):
    out_shape = shape_of(ROWS, COLS, LANES)
    return call(ocean_kernel, "ocean", [velocity, stokes, sea], out_shape, [(EXT_R, EXT_C, LANES)], 4)


def body(
    spectrum,
    velocity,
    gain_matrix,
    quad_matrix,
    limiter_flags,
    sea_mask,
    current_route,
    stokes_route,
):
    band_index = lax.axis_index("band")
    freq_index = lax.axis_index("freq")
    chunks = lax.all_to_all(spread(spectrum), "freq", split_axis=0, concat_axis=0, tiled=True)

    tile = jnp.transpose(velocity, (2, 3, 0, 1)).reshape(ROWS, COLS, 2 * LAYERS)
    tile = jnp.pad(tile, ((0, 0), (0, 0), (0, LANES - 2 * LAYERS))).reshape(ROWS * COLS, LANES)

    cos_table, sin_table = directions(DIR)
    speeds = speed_of(jnp.arange(FREQS, dtype=jnp.int32), FREQS)
    waves = 0.5 * speeds[None, :, None] * jnp.stack([cos_table, sin_table])[:, None, :]
    waves = waves.reshape(2, 1, COMP)
    routes = jnp.repeat(current_route, DIR).astype(f32)[None, None, :]
    waves = jnp.concatenate([waves, routes], axis=0)

    def window(grid):
        padded = jnp.pad(grid, ((0, 0), (HALO, HALO), (HALO, HALO))).astype(f32)
        part = lax.dynamic_slice(
            padded,
            (0, band_index * ROWS, freq_index * COLS),
            (grid.shape[0], EXT_R, EXT_C),
        )
        return jnp.broadcast_to(part[..., None], part.shape + (LANES,)).reshape(-1, LANES)

    flags = window(limiter_flags)
    sea = window(sea_mask[None])

    numbers = wavenumber(jnp.arange(FREQS, dtype=jnp.int32), FREQS) * DIR ** (-0.5)
    deposit = deposit_table(stokes_route) * numbers[:, None]
    deposit = jnp.pad(jnp.tile(deposit, (1, 2)), ((0, 0), (0, LANES - 2 * LAYERS)))
    eastward = jnp.arange(LANES) < LAYERS
    angles = jnp.where(eastward[None, :], cos_table[:, None], sin_table[:, None])

    tables = [waves, angles, deposit]
    chunks, tile, flags, sea, tables = lax.optimization_barrier((chunks, tile, flags, sea, tables))
    fixed = [flags, sea, gain_matrix, quad_matrix]
    pieces = widen(*unpack(chunks, tile))
    results = run_cycle(True, [*pieces, *fixed, *tables])
    velocity_ext, faces = results[3], results[4:]
    pieces = widen(*results[:3])
    chunks, stokes_ext = run_cycle(False, [*pieces, *fixed, *faces])
    chunks = lax.all_to_all(chunks, "freq", split_axis=0, concat_axis=0, tiled=True)
    ocean_out = ocean(velocity_ext, stokes_ext, sea)
    ocean_out = ocean_out[:, :, : 2 * LAYERS].reshape(ROWS, COLS, 2, LAYERS)
    velocity_out = jnp.transpose(ocean_out, (2, 3, 0, 1))
    return (collect(chunks), velocity_out)


def solution(mesh):
    return jax.shard_map(
        body,
        mesh=mesh,
        in_specs=(
            P("freq", None, "band", None),
            P(None, None, "band", "freq"),
            P(),
            P(),
            P(),
            P(),
            P(),
            P(),
        ),
        out_specs=(P("freq", None, "band", None), P(None, None, "band", "freq")),
        check_vma=False,
    )
```

```python
import jax
import jax.numpy as jnp
from jax import lax
from jax.experimental import pallas as pl
from jax.experimental.pallas import tpu as pltpu
from jax.sharding import PartitionSpec as P

DIR = 36
FREQS = 32
COMP = 1152
LAYERS = 24
SUB = 4
CYCLES = 2
OSTEPS = 3
BANDS = 8
ROWS = 16
COLS = 8
HALO = 4
EXT_R = 24
EXT_C = 16
LANES = 128
GROUPS = 9
QUADS = COMP // 4
KEPT = 10
MAIN = 8
CELLS = EXT_R * EXT_C

ocean_dt = 0.2
viscous = 0.5
mixing = 0.5
friction = 0.1

f32 = jnp.float32


def directions(how_many):
    angles = (jnp.arange(how_many, dtype=f32) + 0.5) * (2.0 * jnp.pi / how_many)
    return (jnp.cos(angles), jnp.sin(angles))


def speed_of(position, total_count):
    return 0.5 + 0.3 * (position.astype(f32) + 0.5) / total_count


def wavenumber(position, total_count):
    return 0.5 + 1.5 * (position.astype(f32) + 0.5) / total_count


def deposit_table(stokes_route):
    layer_ids = jnp.arange(LAYERS, dtype=jnp.int32)
    weights = 1.0 / (1.0 + jnp.arange(stokes_route.shape[1], dtype=f32))
    hits = (stokes_route[:, :, None] == layer_ids[None, None, :]).astype(f32)
    return jnp.sum(hits * weights[None, :, None], axis=1)


def line(count, shift):
    return [(i, i - shift) for i in range(count) if 0 <= i - shift < count]


def widen(own, to_last, to_next):
    from_next = lax.ppermute(to_last, "freq", line(FREQS, 1))
    from_last = lax.ppermute(to_next, "freq", line(FREQS, -1))
    first, last = ends(own, from_next, from_last)
    from_up = lax.ppermute(first, "band", line(BANDS, 1))
    from_down = lax.ppermute(last, "band", line(BANDS, -1))
    return [own, from_next, from_last, from_up, from_down]


def block(row, group, cols):
    start = (row * KEPT + group) * cols
    return slice(start, start + cols)


def fill(ext_ref, pieces, group):
    own, from_next, from_last, from_up, from_down = pieces
    for r in range(ROWS):
        ext_ref[HALO + r, 0:HALO, :] = from_last[block(r, group, HALO), :]
        ext_ref[HALO + r, HALO : HALO + COLS, :] = own[block(r, group, COLS), :]
        ext_ref[HALO + r, HALO + COLS : EXT_C, :] = from_next[block(r, group, HALO), :]
    for r in range(HALO):
        ext_ref[HALO + ROWS + r] = from_up[block(r, group, EXT_C), :]
        ext_ref[r] = from_down[block(r, group, EXT_C), :]


def fill_cells(cell_ref, pieces):
    own, from_next, from_last, from_up, from_down = pieces

    def take(ref, row, col, cols, ext_row, ext_col):
        start = (ext_row * EXT_C + ext_col) * MAIN
        cell_ref[start : start + MAIN, :] = ref[pl.ds(row * KEPT * cols + col, MAIN, stride=cols), :]

    for r in range(ROWS):
        for c in range(COLS):
            take(own, r, c, COLS, HALO + r, HALO + c)
        for c in range(HALO):
            take(from_next, r, c, HALO, HALO + r, HALO + COLS + c)
            take(from_last, r, c, HALO, HALO + r, c)
    for r in range(HALO):
        for c in range(EXT_C):
            take(from_up, r, c, EXT_C, HALO + ROWS + r, c)
            take(from_down, r, c, EXT_C, r, c)


def swap_blocks(tiles):
    block = lax.broadcasted_iota(jnp.int32, tiles[0].shape, 1) // 8
    for bit in (1, 2, 4, 8):
        upper = (block & bit) != 0
        fresh = list(tiles)
        for low in range(16):
            if low & bit:
                continue
            high = low | bit
            fresh[low] = jnp.where(upper, pltpu.roll(tiles[high], bit * 8, 1), tiles[low])
            fresh[high] = jnp.where(upper, tiles[high], pltpu.roll(tiles[low], LANES - bit * 8, 1))
        tiles = fresh
    return tiles


def direction_groups():
    for index in range(5):
        count = min(8, DIR - 8 * index)
        for half in range(2):
            yield index, count, half, 2 * index + half


def rows_copy(hbm_ref, vmem_ref, sems, group, outward):
    index, count, half, slot = group
    far = hbm_ref.at[pl.ds(index * 8 * ROWS, count * ROWS), pl.ds(half * LANES, LANES)]
    near = vmem_ref.at[slot, pl.ds(0, count * ROWS)]
    pair = (near, far) if outward else (far, near)
    return pltpu.make_async_copy(*pair, sems.at[slot])


def spread_kernel(x_hbm, o_hbm, half_ref, chunk_ref, in_sems, out_sems):
    groups = list(direction_groups())
    copies = [rows_copy(x_hbm, half_ref, in_sems, group, False) for group in groups]
    for copy in copies:
        copy.start()
    sent = []
    for batch, quads in ((groups[:6], pl.ds(0, 6)), (groups[6:], pl.ds(6, 3))):
        for group in batch:
            copies[group[3]].wait()
        for index, count, half, slot in batch:
            tiles = [half_ref[slot, pl.ds(r, count, stride=ROWS), :] for r in range(ROWS)]
            for i, tile in enumerate(swap_blocks(tiles)):
                for j in range(count // 4):
                    chunk_ref[half * ROWS + i, 2 * index + j] = tile[4 * j : 4 * j + 4]
        far = o_hbm.at[:, quads]
        sent.append(pltpu.make_async_copy(chunk_ref.at[:, quads], far, out_sems.at[len(sent)]))
        sent[-1].start()
    for copy in sent:
        copy.wait()


def collect_kernel(x_ref, o_hbm, half_ref, sems):
    groups = list(direction_groups())
    copies = []
    for batch in (groups[:6], groups[6:]):
        for index, count, half, slot in batch:
            tiles = []
            for i in range(ROWS):
                quads = [x_ref[half * ROWS + i, 2 * index + j] for j in range(count // 4)]
                tiles.append(jnp.concatenate(quads, axis=0))
            for r, tile in enumerate(swap_blocks(tiles)):
                half_ref[slot, pl.ds(r, count, stride=ROWS), :] = tile
        for group in batch:
            copies.append(rows_copy(o_hbm, half_ref, sems, group, True))
            copies[-1].start()
    for copy in copies:
        copy.wait()


def ends_kernel(own, from_next, from_last, first_ref, last_ref):
    for ref, start in ((first_ref, 0), (last_ref, ROWS - HALO)):
        for r in range(HALO):
            for k in range(KEPT):
                at = block(r, k, EXT_C).start
                ref[at : at + HALO, :] = from_last[block(start + r, k, HALO), :]
                ref[at + HALO : at + HALO + COLS, :] = own[block(start + r, k, COLS), :]
                ref[at + HALO + COLS : at + EXT_C, :] = from_next[block(start + r, k, HALO), :]


def put(value, refs, group):
    for r in range(ROWS):
        row = value[r * COLS : (r + 1) * COLS, :]
        refs[0][block(r, group, COLS), :] = row
        refs[1][block(r, group, HALO), :] = row[:HALO]
        refs[2][block(r, group, HALO), :] = row[HALO:]


def unpack_kernel(x_ref, u_ref, *rest):
    out_refs, flat_ref = rest[:-1], rest[-1]
    for q in range(QUADS):
        flat_ref[4 * q : 4 * q + 4, :] = x_ref[q]
    for k in range(GROUPS):
        put(jnp.transpose(flat_ref[k * LANES : (k + 1) * LANES, :]), out_refs, k)
    put(u_ref[...], out_refs, GROUPS)


def face_flux(lower, upper, half_courant, half_square, second):
    q = jnp.where(second, half_square, jnp.abs(half_courant))
    return lower * (half_courant + q) + upper * (half_courant - q)


def courants(ext_ref, lane_ref, main_ref, rest_ref):
    lane = lax.broadcasted_iota(jnp.int32, (EXT_C, LANES), 1)
    quarter = (0.25 * 0.15) * jnp.tanh(ext_ref[...])
    faces = []
    for r in range(EXT_R):
        along_rows = quarter[r] + quarter[min(r + 1, EXT_R - 1)]
        along_cols = quarter[r] + pltpu.roll(quarter[r], 1, 0)
        faces.append(jnp.where(lane < LAYERS, along_cols, along_rows))
    faces = jnp.concatenate(faces, axis=0)
    high = faces.astype(jnp.bfloat16).astype(f32)
    rest = faces - high
    middle = rest.astype(jnp.bfloat16).astype(f32)
    parts = jnp.concatenate([high + pltpu.roll(middle, LANES // 2, 1), rest - middle], axis=1)
    parts = parts.astype(jnp.bfloat16)
    layer = lax.broadcasted_iota(jnp.int32, (2 * LAYERS, LANES), 0).astype(f32)
    blank = jnp.zeros((LANES, LANES), f32)
    short, long = blank[: LANES // 2 - 2 * LAYERS], blank[: LANES - 2 * LAYERS]
    for index in range(2):
        for k in range(GROUPS):
            lanes = slice(k * LANES, (k + 1) * LANES)
            hit = jnp.where(layer == lane_ref[2, :, lanes] + LAYERS * index, 1.0, 0.0)
            picker = jnp.concatenate([hit, short, hit, short, hit, long], axis=0)
            picked = jnp.dot(parts, picker.astype(jnp.bfloat16), preferred_element_type=f32)
            half_courant = lane_ref[index, :, lanes] + picked
            square = (half_courant + half_courant) * half_courant
            for which, value in ((2 * index, half_courant), (2 * index + 1, square)):
                if k == MAIN:
                    rest_ref[which] = value.reshape(EXT_R, EXT_C, LANES)
                    continue
                for start in range(0, CELLS, 8):
                    at = (which * CELLS + start) * MAIN + k
                    main_ref[pl.ds(at, 8, stride=MAIN), :] = value[start : start + 8, :]


def advect_cells(cell_ref, face_ref, flag_ref, sea_ref, energy_ref, flag_base):
    def at(start):
        return pl.ds(start * MAIN, MAIN)

    def cell(r, c):
        return cell_ref[at(r * EXT_C + c), :]

    def flux(lower, upper, which, r, c, flag_row):
        half_courant = face_ref[at(which * CELLS + r * EXT_C + c), :]
        half_square = face_ref[at((which + 1) * CELLS + r * EXT_C + c), :]
        second = flag_ref[pl.ds(flag_row * EXT_C + c, MAIN, stride=0), :] != 0.0
        return face_flux(lower, upper, half_courant, half_square, second)

    for s in range(SUB):
        cols = range(s, EXT_C - s)
        flag_top = (flag_base + s) * EXT_R

        def upper_flux(r, c):
            return flux(cell(r, c), cell(r + 1, c), 2, r, c, flag_top + r + 1)

        def row(r, below):
            above = [upper_flux(r, c) for c in cols]
            shifted = [cell(r, c) - (a - b) for c, a, b in zip(cols, above, below)]
            along = [
                flux(shifted[i - 1], shifted[i], 0, r, cols[i], flag_top + r)
                for i in range(1, len(cols))
            ]
            for i in range(1, len(cols) - 1):
                sea = sea_ref[pl.ds(r * EXT_C + cols[i], MAIN, stride=0), :]
                result = (shifted[i] - (along[i] - along[i - 1])) * sea
                if s == SUB - 1:
                    start = (r - HALO) * GROUPS * COLS + cols[i] - HALO
                    energy_ref[pl.ds(start, MAIN, stride=COLS), :] = result
                else:
                    cell_ref[at(r * EXT_C + cols[i]), :] = result
            return above

        below = [upper_flux(s, c) for c in cols]
        for r in range(s + 1, EXT_R - 1 - s):
            below = row(r, below)


def advect_rest(tile_ref, face_ref, flag_ref, sea_ref, energy_ref, flag_base):
    def rows_of(ref, r):
        return ref[r * EXT_C : (r + 1) * EXT_C, :]

    for s in range(SUB):
        flag_top = (flag_base + s) * EXT_R
        here = tile_ref[s]
        above = tile_ref[s + 1]
        flag = rows_of(flag_ref, flag_top + s + 1) != 0.0
        flux_below = face_flux(here, above, face_ref[2, s], face_ref[3, s], flag)
        for r in range(s + 1, EXT_R - 1 - s):
            here = above
            above = tile_ref[r + 1]
            flag_above = rows_of(flag_ref, flag_top + r + 1) != 0.0
            flux_above = face_flux(here, above, face_ref[2, r], face_ref[3, r], flag_above)
            shifted = here - (flux_above - flux_below)
            flux_east = face_flux(
                pltpu.roll(shifted, 1, 0), shifted, face_ref[0, r], face_ref[1, r], flag
            )
            result = shifted - (pltpu.roll(flux_east, EXT_C - 1, 0) - flux_east)
            result = result * rows_of(sea_ref, r)
            if s == SUB - 1:
                start = ((r - HALO) * GROUPS + MAIN) * COLS
                energy_ref[start : start + COLS, :] = result[HALO : HALO + COLS]
            else:
                tile_ref[r] = result
            flux_below = flux_above
            flag = flag_above


def stokes_weights(angle_ref, deposit_ref, weight_ref):
    for g in range(FREQS):
        rows = angle_ref[...] * deposit_ref[g : g + 1, :]
        for d in range(0, DIR, 4):
            weight_ref[g * DIR + d : g * DIR + d + 4, :] = rows[d : d + 4]


def cycle_kernel(first, *refs):
    refs = list(refs)
    take = lambda n: [refs.pop(0) for _ in range(n)]
    pieces = take(5)
    flag_ref, sea_ref, gain_ref, quad_ref = take(4)
    flag_base = 0 if first else SUB
    if first:
        lane_ref, angle_ref, deposit_ref = take(3)
        out_refs = take(3)
        (ext_ref,) = take(1)
        main_ref, rest_ref = take(2)
    else:
        main_ref, rest_ref = take(2)
        out_hbm, ext_ref = take(2)
    cell_ref, tile_ref, energy_ref = take(3)
    if first:
        (weight_ref,) = take(1)
        stokes_weights(angle_ref, deposit_ref, weight_ref)
    else:
        chunk_ref, sems = take(2)
    fill(ext_ref, pieces, GROUPS)
    if first:
        courants(ext_ref, lane_ref, main_ref, rest_ref)
    fill_cells(cell_ref, pieces)
    fill(tile_ref, pieces, MAIN)
    advect_rest(tile_ref, rest_ref, flag_ref, sea_ref, energy_ref, flag_base)
    advect_cells(cell_ref, main_ref, flag_ref, sea_ref, energy_ref, flag_base)

    def energy_group(k):
        starts = [(r * GROUPS + k) * COLS for r in range(ROWS)]
        return jnp.concatenate([energy_ref[a : a + COLS, :] for a in starts], axis=0)

    copies = []
    energy = jnp.concatenate([energy_group(k) for k in range(GROUPS)], axis=1)
    rounded = energy.astype(jnp.bfloat16)
    squared = (energy * energy).astype(jnp.bfloat16)
    if first:
        rest = (energy - rounded.astype(f32)).astype(jnp.bfloat16)
        mm = lambda a, b: jnp.dot(a, b, preferred_element_type=f32)
        weight = weight_ref[...]
        weight_hi = weight.astype(jnp.bfloat16)
        weight_lo = (weight - weight_hi.astype(f32)).astype(jnp.bfloat16)
        stokes = mm(rounded, weight_hi) + (mm(rest, weight_hi) + mm(rounded, weight_lo))
        put(stokes, out_refs, GROUPS)
    nt = (((1,), (1,)), ((), ()))
    for k in range(GROUPS):
        lanes = pl.ds(k * LANES, LANES)
        gain = lax.dot_general(rounded, gain_ref[lanes, :], nt, preferred_element_type=f32)
        quartic = lax.dot_general(squared, quad_ref[lanes, :], nt, preferred_element_type=f32)
        updated = energy_group(k) * (1.0 + 0.5 * jnp.tanh(gain) - 0.25 * jnp.tanh(quartic))
        if first:
            put(updated, out_refs, k)
        else:
            flat = jnp.transpose(updated)
            for q in range(32):
                chunk_ref[32 * k + q] = flat[4 * q : 4 * q + 4]
            part = pl.ds(32 * k, 32)
            copies.append(pltpu.make_async_copy(chunk_ref.at[part], out_hbm.at[part], sems.at[k]))
            copies[-1].start()
    for copy in copies:
        copy.wait()


def ocean_kernel(u_ref, drift_ref, sea_ref, o_ref, now_ref):
    now_ref[...] = u_ref[...]
    lane = lax.broadcasted_iota(jnp.int32, (EXT_C, LANES), 1)
    used = lane < 2 * LAYERS
    east = lane < LAYERS
    top = (lane == LAYERS - 1) | (lane == 2 * LAYERS - 1)
    bottom = (lane == 0) | (lane == LAYERS)
    for s in range(OSTEPS):
        low = 2 + s
        below = now_ref[low - 1]
        here = now_ref[low]
        for r in range(low, EXT_R - low):
            above = now_ref[r + 1]
            laplace = above + below + pltpu.roll(here, EXT_C - 1, 0) + pltpu.roll(here, 1, 0) - 4.0 * here
            moving = here + drift_ref[r]
            turning = jnp.where(
                east, pltpu.roll(moving, LANES - LAYERS, 1), -pltpu.roll(moving, LAYERS, 1)
            )
            over = jnp.where(top, 0.0, pltpu.roll(here, LANES - 1, 1))
            under = jnp.where(bottom, 0.0, pltpu.roll(here, 1, 1))
            tendency = (
                viscous * laplace + turning + mixing * (over + under - 2.0 * here) - friction * here
            )
            result = jnp.where(used, (here + ocean_dt * tendency) * sea_ref[r * EXT_C : (r + 1) * EXT_C, :], 0.0)
            if s == OSTEPS - 1:
                o_ref[r - HALO] = result[HALO : HALO + COLS]
            else:
                now_ref[r] = result
            below, here = here, above


def shape_of(*dims, dtype=f32):
    return jax.ShapeDtypeStruct(dims, dtype)


vmem = pl.BlockSpec(memory_space=pltpu.VMEM)
hbm = pl.BlockSpec(memory_space=pltpu.HBM)


def call(kernel, name, operands, out_shape, scratch, mebibytes, in_specs=None, out_specs=None):
    return pl.pallas_call(
        kernel,
        out_shape=out_shape,
        in_specs=in_specs or [vmem] * len(operands),
        out_specs=out_specs or jax.tree.map(lambda _: vmem, out_shape),
        scratch_shapes=[pltpu.VMEM(x, f32) if isinstance(x, tuple) else x for x in scratch],
        compiler_params=pltpu.CompilerParams(vmem_limit_bytes=mebibytes * 2**20),
        name=name,
    )(*operands)


halves = (10, 8 * ROWS, LANES)
chunks_dims = (FREQS, DIR // 4, 4, LANES)
sems = pltpu.SemaphoreType.DMA


def spread(x):
    x = x.reshape(DIR * ROWS, 2 * LANES)
    scratch = [halves, chunks_dims, sems((10,)), sems((2,))]
    out = call(spread_kernel, "spread", [x], shape_of(*chunks_dims), scratch, 4, [hbm], hbm)
    return out.reshape(QUADS, 4, LANES)


def collect(x):
    out_shape = shape_of(DIR * ROWS, 2 * LANES)
    scratch = [halves, sems((10,))]
    x = x.reshape(chunks_dims)
    out = call(collect_kernel, "collect", [x], out_shape, scratch, 4, [vmem], hbm)
    return out.reshape(1, DIR, ROWS, 2 * LANES)


tile_shapes = [shape_of(ROWS * KEPT * COLS, LANES)] + [shape_of(ROWS * KEPT * HALO, LANES)] * 2
ext_shape = shape_of(EXT_R, EXT_C, LANES)


def unpack(x, velocity):
    return call(unpack_kernel, "unpack", [x, velocity], tile_shapes, [(COMP, LANES)], 8)


def ends(*pieces):
    return call(ends_kernel, "ends", pieces, [shape_of(HALO * KEPT * EXT_C, LANES)] * 2, [], 4)


def run_cycle(first, operands):
    scratch = [(CELLS * MAIN, LANES), (EXT_R, EXT_C, LANES), (ROWS * GROUPS * COLS, LANES)]
    if first:
        faces = [shape_of(4 * CELLS * MAIN, LANES), shape_of(4, EXT_R, EXT_C, LANES)]
        out_shape = tile_shapes + [ext_shape] + faces
        scratch += [(COMP, LANES)]
        out_specs = [vmem] * 6
    else:
        out_shape = [shape_of(QUADS, 4, LANES), ext_shape]
        out_specs = [hbm, vmem]
        scratch += [(QUADS, 4, LANES), sems((GROUPS,))]
    kernel = lambda *refs: cycle_kernel(first, *refs)
    name = "cycle_first" if first else "cycle_last"
    return call(kernel, name, operands, out_shape, scratch, 20, None, out_specs)


def ocean(velocity, stokes, sea):
    out_shape = shape_of(ROWS, COLS, LANES)
    return call(ocean_kernel, "ocean", [velocity, stokes, sea], out_shape, [(EXT_R, EXT_C, LANES)], 4)


def body(
    spectrum,
    velocity,
    gain_matrix,
    quad_matrix,
    limiter_flags,
    sea_mask,
    current_route,
    stokes_route,
):
    band_index = lax.axis_index("band")
    freq_index = lax.axis_index("freq")
    chunks = lax.all_to_all(spread(spectrum), "freq", split_axis=0, concat_axis=0, tiled=True)

    tile = jnp.transpose(velocity, (2, 3, 0, 1)).reshape(ROWS, COLS, 2 * LAYERS)
    tile = jnp.pad(tile, ((0, 0), (0, 0), (0, LANES - 2 * LAYERS))).reshape(ROWS * COLS, LANES)

    cos_table, sin_table = directions(DIR)
    speeds = speed_of(jnp.arange(FREQS, dtype=jnp.int32), FREQS)
    waves = 0.5 * speeds[None, :, None] * jnp.stack([cos_table, sin_table])[:, None, :]
    waves = waves.reshape(2, 1, COMP)
    routes = jnp.repeat(current_route, DIR).astype(f32)[None, None, :]
    waves = jnp.concatenate([waves, routes], axis=0)

    def window(grid):
        padded = jnp.pad(grid, ((0, 0), (HALO, HALO), (HALO, HALO))).astype(f32)
        part = lax.dynamic_slice(
            padded,
            (0, band_index * ROWS, freq_index * COLS),
            (grid.shape[0], EXT_R, EXT_C),
        )
        return jnp.broadcast_to(part[..., None], part.shape + (LANES,)).reshape(-1, LANES)

    flags = window(limiter_flags)
    sea = window(sea_mask[None])

    numbers = wavenumber(jnp.arange(FREQS, dtype=jnp.int32), FREQS) * DIR ** (-0.5)
    deposit = deposit_table(stokes_route) * numbers[:, None]
    deposit = jnp.pad(jnp.tile(deposit, (1, 2)), ((0, 0), (0, LANES - 2 * LAYERS)))
    eastward = jnp.arange(LANES) < LAYERS
    angles = jnp.where(eastward[None, :], cos_table[:, None], sin_table[:, None])

    tables = [waves, angles, deposit]
    chunks, tile, flags, sea, tables = lax.optimization_barrier((chunks, tile, flags, sea, tables))
    fixed = [flags, sea, gain_matrix, quad_matrix]
    pieces = widen(*unpack(chunks, tile))
    results = run_cycle(True, [*pieces, *fixed, *tables])
    velocity_ext, faces = results[3], results[4:]
    pieces = widen(*results[:3])
    chunks, stokes_ext = run_cycle(False, [*pieces, *fixed, *faces])
    chunks = lax.all_to_all(chunks, "freq", split_axis=0, concat_axis=0, tiled=True)
    ocean_out = ocean(velocity_ext, stokes_ext, sea)
    ocean_out = ocean_out[:, :, : 2 * LAYERS].reshape(ROWS, COLS, 2, LAYERS)
    velocity_out = jnp.transpose(ocean_out, (2, 3, 0, 1))
    return (collect(chunks), velocity_out)


def solution(mesh):
    return jax.shard_map(
        body,
        mesh=mesh,
        in_specs=(
            P("freq", None, "band", None),
            P(None, None, "band", "freq"),
            P(),
            P(),
            P(),
            P(),
            P(),
            P(),
        ),
        out_specs=(P("freq", None, "band", None), P(None, None, "band", "freq")),
        check_vma=False,
    )
```
